32 devices in a mesh: col: 4 (over x, core), slab: 8 (over z, y).
Axes of the slice: x: 2, y: 2, z: 4, core: 2. Of those that a mesh axis runs over, the one named last changes fastest.
Arguments:
- labels: int32 [32, 64, 128], P('col', 'slab'), may hold values from 0 to 2
- table: float32 [3], replicated, may hold values from 0.3 to 3
- factor: float32 [32, 64, 128], P('col', 'slab'), may hold values from 0.5 to 2
- chi: float32 [3, 32, 64, 128], P(None, 'col', 'slab'), may hold values from -2.5 to 2.5
- weights: float32 [3, 3], replicated, may hold values from -3.5 to 3.5
Outputs:
- adjoint: float32 [3, 32, 64, 128], P(None, 'col', 'slab')
- gradient: float32 [32, 64, 128], P('col', 'slab')
The draws below stay inside these ranges and needn't reach their ends.
All inputs are finite; a program needn't handle non-finite values.
Results may differ from the reference program's by a relative error of at most 0.0001.
Values sent between devices are 32-bit elements; how exact they have to be, the bound alone decides.
No kernel may reach another device: no remote copies, remote signals or barrier semaphores. Data moves between devices by JAX's collectives and lax.ppermute only.
A program may use at most 64 MiB of HBM per device.

```python
import math
import jax
import jax.numpy as jnp

NY = 128
ITERS = 3
NX = 32
NZ = 64


def touch_ends(values, key, low, top_value):
    longest = values.shape.index(max(values.shape))
    spots = []
    for shift in (0, 1):
        where = [jax.random.randint(jax.random.fold_in(key, axis), (), 0, length) for axis, length in enumerate(values.shape)]
        where[longest] = (where[longest] + shift) % values.shape[longest]
        spots.append(tuple(where))
    return values.at[spots[0]].set(low).at[spots[1]].set(top_value)


def block_levels(rng, extent, split, smallest, top_value):
    loudness, own = 1.0, jax.random.fold_in(rng, 6)
    for position, parts in split:
        draws = jnp.exp(jax.random.uniform(jax.random.fold_in(own, position), (parts,), jnp.float32, smallest / len(split), top_value / len(split)))
        loudness = loudness * jnp.repeat(draws, extent[position] // parts).reshape([-1 if axis == position else 1 for axis in range(len(extent))])
    return loudness


def normal_values(stream_key, dims, width, reach, pieces=(), held_as=jnp.bfloat16):
    drawn = jax.random.normal(stream_key, dims, jnp.float32) * width
    if len(pieces) > 0:
        drawn = block_levels(stream_key, dims, pieces, -0.22, 0.18) * drawn
    return jnp.clip(drawn, min=-reach, max=reach).astype(held_as)


def setup_inputs(seed: int = 0) -> dict:
    seeds = jax.random.split(jax.random.key(seed), 6)
    labels = touch_ends(jax.random.randint(seeds[0], (NX, NZ, NY), 0, 3), jax.random.fold_in(seeds[0], 1), 0, 2).astype(jnp.int32)
    table = jnp.clip(jnp.exp(jax.random.uniform(seeds[1], (3,), jnp.float32, math.log(0.3), math.log(3.0))), 0.3, 3.0)
    factor = jnp.clip(jnp.exp(math.log(2.0) - 1.3862944 * jax.random.uniform(seeds[2], (NX, NZ, NY), jnp.float32) ** block_levels(seeds[2], (NX, NZ, NY), ((0, 4), (1, 8)), -0.2, 0.2)), 0.5, 2.0)
    chi = normal_values(seeds[3], (3, NX, NZ, NY), 0.3, 2.5, ((1, 4), (2, 8)), jnp.float32)
    weights = normal_values(seeds[4], (3, 3), 3 ** -0.5, 3.5, (), jnp.float32)
    return dict(labels=labels, table=table, factor=factor, chi=chi, weights=weights)


mass_shift = 0.01


def forward_pair(field, spatial):
    return field, jnp.roll(field, -1, axis=spatial - 3)


def back_shift(field, spatial):
    return jnp.roll(field, 1, axis=spatial - 3)


def widen(values):
    return values[:, None, None, None]


def reference(labels, table, factor, chi, weights):
    conduct = table[labels] * factor
    cond, strain, kpairs = [], [], []
    for d in range(3):
        here, after = forward_pair(conduct, d)
        cond.append(2.0 * here * after / (here + after))
        kpairs.append((here, after))
        c_here, c_after = forward_pair(chi, d)
        strain.append(jnp.stack([(1.0 if j == d else 0.0) + (c_after[j] - c_here[j]) for j in range(3)]))
    drive = jnp.zeros_like(chi)
    for d in range(3):
        flux = cond[d] * strain[d]
        drive = drive + (back_shift(flux, d) - flux)
    source = jnp.stack([weights[i, 0] * drive[0] + weights[i, 1] * drive[1] + weights[i, 2] * drive[2] for i in range(3)])

    def apply_operator(field):
        result = mass_shift * field
        for d in range(3):
            after = jnp.roll(field, -1, axis=d - 3)
            before = jnp.roll(field, 1, axis=d - 3)
            result = result + cond[d] * (field - after) + back_shift(cond[d], d) * (field - before)
        return result

    adjoint = jnp.zeros_like(source)
    residual = source
    direction = source
    norm_now = jnp.sum(residual * residual, axis=(1, 2, 3))
    for step in range(ITERS):
        image = apply_operator(direction)
        alpha = norm_now / jnp.sum(direction * image, axis=(1, 2, 3))
        adjoint = adjoint + widen(alpha) * direction
        residual = residual - widen(alpha) * image
        norm_next = jnp.sum(residual * residual, axis=(1, 2, 3))
        direction = residual + widen(norm_next / norm_now) * direction
        norm_now = norm_next

    gradient = jnp.zeros_like(conduct)
    for d in range(3):
        lam_here, lam_after = forward_pair(adjoint, d)
        lam_diff = lam_after - lam_here
        local = strain[d]
        energy = jnp.zeros_like(conduct)
        for i in range(3):
            for j in range(3):
                energy = energy + weights[i, j] * local[i] * local[j]
        h_term = energy - (lam_diff[0] * local[0] + lam_diff[1] * local[1] + lam_diff[2] * local[2])
        here, after = kpairs[d]
        square_sum = (here + after) ** 2
        part_here = 2.0 * after * after / square_sum
        part_after = 2.0 * here * here / square_sum
        gradient = gradient + h_term * part_here + back_shift(h_term * part_after, d)
    return adjoint, gradient
```

```python
import functools

import jax
import jax.numpy as jnp
from jax import lax
from jax.experimental import pallas as pl
from jax.experimental.pallas import tpu as pltpu
from jax.sharding import PartitionSpec as P


mass_shift = 0.01
HALO = 4
STEP = 16
MOMENTS = 6

VMEM = pl.BlockSpec(memory_space=pltpu.VMEM)
SMEM = pl.BlockSpec(memory_space=pltpu.SMEM)


def tile_iota(axis):
    return lax.broadcasted_iota(jnp.int32, (8, 128), axis)


def y_next(tile):
    return pltpu.roll(tile, 127, 1)


def y_prev(tile):
    return pltpu.roll(tile, 1, 1)


def z_next(pair):
    last = tile_iota(0) == 7
    first, second = (pltpu.roll(tile, 7, 0) for tile in pair)
    return jnp.where(last, second, first), jnp.where(last, first, second)


def z_prev(pair):
    top = tile_iota(0) == 0
    first, second = (pltpu.roll(tile, 1, 0) for tile in pair)
    return jnp.where(top, second, first), jnp.where(top, first, second)


def prepare(labels, table, factor, chi, weights, own, low_rows, high_rows, splat):
    layers = factor.shape[0]
    for x in range(layers):
        label = labels[x]
        conduct = jnp.where(label == 0, table[0], jnp.where(label == 1, table[1], table[2])) * factor[x]
        own[3, x] = conduct
        for j in range(3):
            own[j, x] = chi[j, x]
    for i in range(3):
        for j in range(3):
            splat[3 * i + j] = jnp.full((8, 128), weights[i, j], jnp.float32)
    half = tile_iota(0) < 4
    for f in range(4):
        for i in range(layers // 2):
            even, odd = own[f, 2 * i], own[f, 2 * i + 1]
            low_rows[f, i] = jnp.where(half, even, pltpu.roll(odd, 4, 0))
            high_rows[f, i] = jnp.where(half, pltpu.roll(even, 4, 0), odd)


def krylov(layers, peers, own, z_low, z_high, x_low, x_high, splat, near, basis, sums, ring, cond, field):
    total = layers + 2 * HALO
    half = tile_iota(0) < 4

    def ring_tiles(f, low, high, i):
        up, down = high[f, i] if not callable(high) else high(f, i), low[f, i] if not callable(low) else low(f, i)
        return jnp.where(half, up, pltpu.roll(down, 4, 0)), jnp.where(half, pltpu.roll(up, 4, 0), down)

    pairs = HALO // 2
    for f in range(4):
        for i in range(layers // 2):
            ring[f, HALO + 2 * i], ring[f, HALO + 2 * i + 1] = ring_tiles(f, z_low, z_high, i)
        for block, start in ((x_low, 0), (x_high, HALO + layers)):
            for i in range(pairs):
                ring[f, start + 2 * i], ring[f, start + 2 * i + 1] = ring_tiles(
                    f, lambda g, k: block[g, HALO + k], lambda g, k: block[g, HALO + pairs + k], i
                )

    def grid(f, x):
        if x < HALO:
            return x_low[f, x], ring[f, x]
        if x >= HALO + layers:
            return x_high[f, x - HALO - layers], ring[f, x]
        return own[f, x - HALO], ring[f, x]

    def harmonic(here, after):
        return 2.0 * here * after / (here + after)

    for x in range(total - 1):
        here = grid(3, x)
        after = grid(3, x + 1)
        beside = z_next(here)
        for t in range(2):
            cond[0, x, t] = harmonic(here[t], after[t])
            cond[1, x, t] = harmonic(here[t], beside[t])
            cond[2, x, t] = harmonic(here[t], y_next(here[t]))

    def out_flow(x, here, after, offset, flows):
        beside = z_next(here)
        added = []
        z_flux = []
        for t in range(2):
            z_flux.append(cond[1, x, t] * (offset[1] + (beside[t] - here[t])))
        z_back = z_prev(z_flux)
        for t in range(2):
            x_flux = cond[0, x, t] * (offset[0] + (after[t] - here[t]))
            y_flux = cond[2, x, t] * (offset[2] + (y_next(here[t]) - here[t]))
            before = flows[t]
            flows[t] = x_flux
            if before is not None:
                added.append((before - x_flux) + (z_back[t] - z_flux[t]) + (y_prev(y_flux) - y_flux))
        return added

    flows = [[None, None] for _ in range(3)]
    for j in range(3):
        for t in range(2):
            here, after = grid(j, 0)[t], grid(j, 1)[t]
            flows[j][t] = cond[0, 0, t] * ((1.0 if j == 0 else 0.0) + (after - here))
    for x in range(1, total - 1):
        drive = []
        for j in range(3):
            offset = [1.0 if d == j else 0.0 for d in range(3)]
            drive.append(out_flow(x, grid(j, x), grid(j, x + 1), offset, flows[j]))
        for i in range(3):
            for t in range(2):
                field[0, i, x, t] = (
                    splat[3 * i] * drive[0][t] + splat[3 * i + 1] * drive[1][t] + splat[3 * i + 2] * drive[2][t]
                )

    for k in (1, 2):
        for i in range(3):
            first = k
            flow = [cond[0, first, t] * (field[k - 1, i, first + 1, t] - field[k - 1, i, first, t]) for t in range(2)]
            for x in range(first + 1, total - 1 - k):
                here = (field[k - 1, i, x, 0], field[k - 1, i, x, 1])
                after = (field[k - 1, i, x + 1, 0], field[k - 1, i, x + 1, 1])
                added = out_flow(x, here, after, (0.0, 0.0, 0.0), flow)
                for t in range(2):
                    field[k, i, x, t] = mass_shift * here[t] + added[t]

    lane = tile_iota(1)
    packed = jnp.zeros((8, 128), jnp.float32)
    for i in range(3):
        flow = [cond[0, HALO - 1, 0] * (field[2, i, HALO, 0] - field[2, i, HALO - 1, 0]), jnp.zeros((8, 128), jnp.float32)]
        partial = [jnp.zeros((8, 128), jnp.float32) for _ in range(MOMENTS)]
        for x in range(HALO, HALO + layers):
            here = (field[2, i, x, 0], field[2, i, x, 1])
            after = (field[2, i, x + 1, 0], field[2, i, x + 1, 1])
            added = out_flow(x, here, after, (0.0, 0.0, 0.0), flow)
            v = [field[0, i, x, 0], field[1, i, x, 0], here[0], mass_shift * here[0] + added[0]]
            for m, (a, b) in enumerate(((0, 0), (0, 1), (1, 1), (1, 2), (2, 2), (2, 3))):
                partial[m] = partial[m] + v[a] * v[b]
        for m in range(MOMENTS):
            packed = jnp.where(lane == STEP * m + i, jnp.sum(partial[m], axis=1, keepdims=True), packed)
    row = jnp.sum(packed, axis=0, keepdims=True)
    sums[...] = jnp.broadcast_to(row, (peers, 128))

    for x in range(layers + 2):
        for t in range(2):
            for f in range(4):
                near[f, x, t] = grid(f, x + HALO - 1)[t]
            for k in range(3):
                for i in range(3):
                    basis[k, i, x, t] = field[k, i, x + HALO - 1, t]


def coefficients(sums):
    row = jnp.broadcast_to(jnp.sum(sums[...], axis=0, keepdims=True), (8, 128))
    m0, m1, m2, m3, m4, m5 = [row if m == 0 else pltpu.roll(row, 128 - STEP * m, 1) for m in range(MOMENTS)]
    alpha0 = m0 / m1
    norm1 = alpha0 * (alpha0 * m2 - m1)
    grow = 1.0 + norm1 / m0
    alpha1 = norm1 / (grow * grow * m1 - 2.0 * grow * alpha0 * m2 + alpha0 * alpha0 * m3)
    r1 = -(alpha0 + alpha1 * grow)
    r2 = alpha1 * alpha0
    norm2 = m0 + 2.0 * r1 * m1 + (r1 * r1 + 2.0 * r2) * m2 + 2.0 * r1 * r2 * m3 + r2 * r2 * m4
    beta1 = norm2 / norm1
    p0, p1, p2 = 1.0 + beta1 * grow, r1 - beta1 * alpha0, r2
    curve2 = (
        p0 * p0 * m1 + 2.0 * p0 * p1 * m2 + (p1 * p1 + 2.0 * p0 * p2) * m3 + 2.0 * p1 * p2 * m4 + p2 * p2 * m5
    )
    alpha2 = norm2 / curve2
    return alpha0 + alpha1 * grow + alpha2 * p0, alpha2 * p1 - alpha1 * alpha0, alpha2 * p2


def finish(layers, sums, near, basis, splat, adjoint, gradient, lam):
    lane = tile_iota(1)
    scale = []
    for c in coefficients(sums):
        scale.append([jnp.sum(jnp.where(lane == i, c, 0.0), axis=1, keepdims=True) for i in range(3)])
    for i in range(3):
        for x in range(layers + 2):
            for t in range(2):
                if t == 1 and x in (0, layers + 1):
                    continue
                value = scale[0][i] * basis[0, i, x, t] + scale[1][i] * basis[1, i, x, t] + scale[2][i] * basis[2, i, x, t]
                lam[i, x, t] = value
                if t == 0 and 0 < x <= layers:
                    adjoint[i, x - 1] = value

    def face(d, here, after, chi_here, chi_after, lam_here, lam_after):
        local = [(1.0 if j == d else 0.0) + (chi_after[j] - chi_here[j]) for j in range(3)]
        h_term = None
        for i in range(3):
            inner = splat[3 * i] * local[0] + splat[3 * i + 1] * local[1] + splat[3 * i + 2] * local[2]
            part = local[i] * (inner - (lam_after[i] - lam_here[i]))
            h_term = part if h_term is None else h_term + part
        inverse = 1.0 / (here + after)
        share = after * inverse
        rest = here * inverse
        return h_term * (2.0 * share * share), h_term * (2.0 * rest * rest)

    carried = None
    for x in range(layers + 1):
        now, back = face(
            0,
            near[3, x, 0],
            near[3, x + 1, 0],
            [near[j, x, 0] for j in range(3)],
            [near[j, x + 1, 0] for j in range(3)],
            [lam[j, x, 0] for j in range(3)],
            [lam[j, x + 1, 0] for j in range(3)],
        )
        if x > 0:
            total = now + carried
            here = near[3, x, 0]
            chi_here = [near[j, x, 0] for j in range(3)]
            lam_here = [lam[j, x, 0] for j in range(3)]
            y_now, y_back = face(
                2, here, y_next(here), chi_here, [y_next(c) for c in chi_here], lam_here, [y_next(c) for c in lam_here]
            )
            total = total + y_now + y_prev(y_back)
            pair = (here, near[3, x, 1])
            chi_pair = [(near[j, x, 0], near[j, x, 1]) for j in range(3)]
            lam_pair = [(lam[j, x, 0], lam[j, x, 1]) for j in range(3)]
            beside = z_next(pair)
            chi_beside = [z_next(c) for c in chi_pair]
            lam_beside = [z_next(c) for c in lam_pair]
            z_now, z_back = zip(
                *[
                    face(
                        1,
                        pair[t],
                        beside[t],
                        [c[t] for c in chi_pair],
                        [c[t] for c in chi_beside],
                        [c[t] for c in lam_pair],
                        [c[t] for c in lam_beside],
                    )
                    for t in range(2)
                ]
            )
            gradient[x - 1] = total + z_now[0] + z_prev(z_back)[0]
        carried = back


def ring_steps(axis):
    count = lax.axis_size(axis)
    forward = [(i, (i + 1) % count) for i in range(count)]
    return forward, [(target, source) for source, target in forward]


def shards(labels, table, factor, chi, weights):
    layers, rows, columns = factor.shape
    assert rows == 8 and columns == 128 and layers % 2 == 0 and layers >= HALO
    peers = lax.axis_size("col") * lax.axis_size("slab")
    f32 = functools.partial(jax.ShapeDtypeStruct, dtype=jnp.float32)
    pairs = HALO // 2

    own, low_rows, high_rows, splat = pl.pallas_call(
        prepare,
        out_shape=(f32((4, layers, 8, 128)), f32((4, layers // 2, 8, 128)), f32((4, layers // 2, 8, 128)), f32((9, 8, 128))),
        in_specs=[VMEM, SMEM, VMEM, VMEM, SMEM],
        out_specs=(VMEM,) * 4,
        name="prepare",
    )(labels, table, factor, chi, weights)

    forward, backward = ring_steps("slab")
    z_low = lax.ppermute(high_rows, "slab", forward)
    z_high = lax.ppermute(low_rows, "slab", backward)
    forward, backward = ring_steps("col")
    tail = layers // 2 - pairs
    x_low = lax.ppermute(
        jnp.concatenate([own[:, layers - HALO :], z_low[:, tail:], z_high[:, tail:]], axis=1), "col", forward
    )
    x_high = lax.ppermute(jnp.concatenate([own[:, :HALO], z_low[:, :pairs], z_high[:, :pairs]], axis=1), "col", backward)

    total = layers + 2 * HALO
    near, basis, sums = pl.pallas_call(
        functools.partial(krylov, layers, peers),
        out_shape=(f32((4, layers + 2, 2, 8, 128)), f32((3, 3, layers + 2, 2, 8, 128)), f32((peers, 128))),
        in_specs=[VMEM] * 6,
        out_specs=(VMEM,) * 3,
        scratch_shapes=[
            pltpu.VMEM((4, total, 8, 128), jnp.float32),
            pltpu.VMEM((3, total, 2, 8, 128), jnp.float32),
            pltpu.VMEM((3, 3, total, 2, 8, 128), jnp.float32),
        ],
        name="krylov",
    )(own, z_low, z_high, x_low, x_high, splat)

    gathered = lax.all_to_all(sums, ("col", "slab"), 0, 0, tiled=True)

    return pl.pallas_call(
        functools.partial(finish, layers),
        out_shape=(f32((3, layers, 8, 128)), f32((layers, 8, 128))),
        in_specs=[VMEM] * 4,
        out_specs=(VMEM,) * 2,
        scratch_shapes=[pltpu.VMEM((3, layers + 2, 2, 8, 128), jnp.float32)],
        name="finish",
    )(gathered, near, basis, splat)


def solution(mesh):
    in_specs = (
        P("col", "slab", None),
        P(),
        P("col", "slab", None),
        P(None, "col", "slab", None),
        P(),
    )
    out_specs = (P(None, "col", "slab", None), P("col", "slab", None))
    return jax.shard_map(shards, mesh=mesh, in_specs=in_specs, out_specs=out_specs, check_vma=False)
```

```python
import functools

import jax
import jax.numpy as jnp
from jax import lax
from jax.experimental import pallas as pl
from jax.experimental.pallas import tpu as pltpu
from jax.sharding import PartitionSpec as P


mass_shift = 0.01
HALO = 4
STEP = 16
MOMENTS = 6

VMEM = pl.BlockSpec(memory_space=pltpu.VMEM)
HBM = pl.BlockSpec(memory_space=pltpu.HBM)
PARAMS = pltpu.CompilerParams(vmem_limit_bytes=8 * 2**20)


def tile_iota(axis):
    return lax.broadcasted_iota(jnp.int32, (8, 128), axis)


def y_next(tile):
    return pltpu.roll(tile, 127, 1)


def y_prev(tile):
    return pltpu.roll(tile, 1, 1)


def z_next(pair):
    last = tile_iota(0) == 7
    first, second = (pltpu.roll(tile, 7, 0) for tile in pair)
    return jnp.where(last, second, first), jnp.where(last, first, second)


def z_prev(pair):
    top = tile_iota(0) == 0
    first, second = (pltpu.roll(tile, 1, 0) for tile in pair)
    return jnp.where(top, second, first), jnp.where(top, first, second)


def prepare(
    labels_hbm, table_hbm, factor_hbm, chi_hbm, weights_hbm, own, low_rows, high_rows, splat,
    labels, table, factor, weights, sems,
):
    layers = factor.shape[0]
    moves = (
        (labels_hbm, labels),
        (table_hbm, table),
        (factor_hbm, factor),
        (chi_hbm, own.at[pl.ds(0, 3)]),
        (weights_hbm, weights),
    )
    copies = [pltpu.make_async_copy(source, target, sems.at[n]) for n, (source, target) in enumerate(moves)]
    for copy in copies:
        copy.start()
    for copy in copies:
        copy.wait()
    for x in range(layers):
        label = labels[x]
        own[3, x] = jnp.where(label == 0, table[0], jnp.where(label == 1, table[1], table[2])) * factor[x]
    for i in range(3):
        for j in range(3):
            splat[3 * i + j] = jnp.full((8, 128), weights[i, j], jnp.float32)
    half = tile_iota(0) < 4
    for f in range(4):
        for i in range(layers // 2):
            even, odd = own[f, 2 * i], own[f, 2 * i + 1]
            low_rows[f, i] = jnp.where(half, even, pltpu.roll(odd, 4, 0))
            high_rows[f, i] = jnp.where(half, pltpu.roll(even, 4, 0), odd)


def krylov(layers, peers, own, z_low, z_high, x_low, x_high, splat, near, basis, sums, ring, cond, field):
    total = layers + 2 * HALO
    half = tile_iota(0) < 4

    def ring_tiles(f, low, high, i):
        up, down = high[f, i] if not callable(high) else high(f, i), low[f, i] if not callable(low) else low(f, i)
        return jnp.where(half, up, pltpu.roll(down, 4, 0)), jnp.where(half, pltpu.roll(up, 4, 0), down)

    pairs = HALO // 2
    for f in range(4):
        for i in range(layers // 2):
            ring[f, HALO + 2 * i], ring[f, HALO + 2 * i + 1] = ring_tiles(f, z_low, z_high, i)
        for block, start in ((x_low, 0), (x_high, HALO + layers)):
            for i in range(pairs):
                ring[f, start + 2 * i], ring[f, start + 2 * i + 1] = ring_tiles(
                    f, lambda g, k: block[g, HALO + k], lambda g, k: block[g, HALO + pairs + k], i
                )

    def grid(f, x):
        if x < HALO:
            return x_low[f, x], ring[f, x]
        if x >= HALO + layers:
            return x_high[f, x - HALO - layers], ring[f, x]
        return own[f, x - HALO], ring[f, x]

    def harmonic(here, after):
        return 2.0 * here * after / (here + after)

    for x in range(total - 1):
        here = grid(3, x)
        after = grid(3, x + 1)
        beside = z_next(here)
        for t in range(2):
            cond[0, x, t] = harmonic(here[t], after[t])
            cond[1, x, t] = harmonic(here[t], beside[t])
            cond[2, x, t] = harmonic(here[t], y_next(here[t]))

    def out_flow(x, here, after, offset, flows):
        beside = z_next(here)
        added = []
        z_flux = []
        for t in range(2):
            z_flux.append(cond[1, x, t] * (offset[1] + (beside[t] - here[t])))
        z_back = z_prev(z_flux)
        for t in range(2):
            x_flux = cond[0, x, t] * (offset[0] + (after[t] - here[t]))
            y_flux = cond[2, x, t] * (offset[2] + (y_next(here[t]) - here[t]))
            before = flows[t]
            flows[t] = x_flux
            if before is not None:
                added.append((before - x_flux) + (z_back[t] - z_flux[t]) + (y_prev(y_flux) - y_flux))
        return added

    flows = [[None, None] for _ in range(3)]
    for j in range(3):
        for t in range(2):
            here, after = grid(j, 0)[t], grid(j, 1)[t]
            flows[j][t] = cond[0, 0, t] * ((1.0 if j == 0 else 0.0) + (after - here))
    for x in range(1, total - 1):
        drive = []
        for j in range(3):
            offset = [1.0 if d == j else 0.0 for d in range(3)]
            drive.append(out_flow(x, grid(j, x), grid(j, x + 1), offset, flows[j]))
        for i in range(3):
            for t in range(2):
                field[0, i, x, t] = (
                    splat[3 * i] * drive[0][t] + splat[3 * i + 1] * drive[1][t] + splat[3 * i + 2] * drive[2][t]
                )

    for k in (1, 2):
        for i in range(3):
            first = k
            flow = [cond[0, first, t] * (field[k - 1, i, first + 1, t] - field[k - 1, i, first, t]) for t in range(2)]
            for x in range(first + 1, total - 1 - k):
                here = (field[k - 1, i, x, 0], field[k - 1, i, x, 1])
                after = (field[k - 1, i, x + 1, 0], field[k - 1, i, x + 1, 1])
                added = out_flow(x, here, after, (0.0, 0.0, 0.0), flow)
                for t in range(2):
                    field[k, i, x, t] = mass_shift * here[t] + added[t]

    lane = tile_iota(1)
    packed = jnp.zeros((8, 128), jnp.float32)
    for i in range(3):
        flow = [cond[0, HALO - 1, 0] * (field[2, i, HALO, 0] - field[2, i, HALO - 1, 0]), jnp.zeros((8, 128), jnp.float32)]
        partial = [jnp.zeros((8, 128), jnp.float32) for _ in range(MOMENTS)]
        for x in range(HALO, HALO + layers):
            here = (field[2, i, x, 0], field[2, i, x, 1])
            after = (field[2, i, x + 1, 0], field[2, i, x + 1, 1])
            added = out_flow(x, here, after, (0.0, 0.0, 0.0), flow)
            v = [field[0, i, x, 0], field[1, i, x, 0], here[0], mass_shift * here[0] + added[0]]
            for m, (a, b) in enumerate(((0, 0), (0, 1), (1, 1), (1, 2), (2, 2), (2, 3))):
                partial[m] = partial[m] + v[a] * v[b]
        for m in range(MOMENTS):
            packed = jnp.where(lane == STEP * m + i, jnp.sum(partial[m], axis=1, keepdims=True), packed)
    row = jnp.sum(packed, axis=0, keepdims=True)
    sums[...] = jnp.broadcast_to(row, (peers, 128))

    for x in range(layers + 2):
        for t in range(2):
            for f in range(4):
                near[f, x, t] = grid(f, x + HALO - 1)[t]
            for k in range(3):
                for i in range(3):
                    basis[k, i, x, t] = field[k, i, x + HALO - 1, t]


def coefficients(sums):
    row = jnp.broadcast_to(jnp.sum(sums[...], axis=0, keepdims=True), (8, 128))
    m0, m1, m2, m3, m4, m5 = [row if m == 0 else pltpu.roll(row, 128 - STEP * m, 1) for m in range(MOMENTS)]
    alpha0 = m0 / m1
    norm1 = alpha0 * (alpha0 * m2 - m1)
    grow = 1.0 + norm1 / m0
    alpha1 = norm1 / (grow * grow * m1 - 2.0 * grow * alpha0 * m2 + alpha0 * alpha0 * m3)
    r1 = -(alpha0 + alpha1 * grow)
    r2 = alpha1 * alpha0
    norm2 = m0 + 2.0 * r1 * m1 + (r1 * r1 + 2.0 * r2) * m2 + 2.0 * r1 * r2 * m3 + r2 * r2 * m4
    beta1 = norm2 / norm1
    p0, p1, p2 = 1.0 + beta1 * grow, r1 - beta1 * alpha0, r2
    curve2 = (
        p0 * p0 * m1 + 2.0 * p0 * p1 * m2 + (p1 * p1 + 2.0 * p0 * p2) * m3 + 2.0 * p1 * p2 * m4 + p2 * p2 * m5
    )
    alpha2 = norm2 / curve2
    return alpha0 + alpha1 * grow + alpha2 * p0, alpha2 * p1 - alpha1 * alpha0, alpha2 * p2


def finish(layers, sums, near, basis, splat, adjoint, gradient, lam):
    lane = tile_iota(1)
    scale = []
    for c in coefficients(sums):
        scale.append([jnp.sum(jnp.where(lane == i, c, 0.0), axis=1, keepdims=True) for i in range(3)])
    for i in range(3):
        for x in range(layers + 2):
            for t in range(2):
                if t == 1 and x in (0, layers + 1):
                    continue
                value = scale[0][i] * basis[0, i, x, t] + scale[1][i] * basis[1, i, x, t] + scale[2][i] * basis[2, i, x, t]
                lam[i, x, t] = value
                if t == 0 and 0 < x <= layers:
                    adjoint[i, x - 1] = value

    def face(d, here, after, chi_here, chi_after, lam_here, lam_after):
        local = [(1.0 if j == d else 0.0) + (chi_after[j] - chi_here[j]) for j in range(3)]
        h_term = None
        for i in range(3):
            inner = splat[3 * i] * local[0] + splat[3 * i + 1] * local[1] + splat[3 * i + 2] * local[2]
            part = local[i] * (inner - (lam_after[i] - lam_here[i]))
            h_term = part if h_term is None else h_term + part
        inverse = 1.0 / (here + after)
        share = after * inverse
        rest = here * inverse
        return h_term * (2.0 * share * share), h_term * (2.0 * rest * rest)

    carried = None
    for x in range(layers + 1):
        now, back = face(
            0,
            near[3, x, 0],
            near[3, x + 1, 0],
            [near[j, x, 0] for j in range(3)],
            [near[j, x + 1, 0] for j in range(3)],
            [lam[j, x, 0] for j in range(3)],
            [lam[j, x + 1, 0] for j in range(3)],
        )
        if x > 0:
            total = now + carried
            here = near[3, x, 0]
            chi_here = [near[j, x, 0] for j in range(3)]
            lam_here = [lam[j, x, 0] for j in range(3)]
            y_now, y_back = face(
                2, here, y_next(here), chi_here, [y_next(c) for c in chi_here], lam_here, [y_next(c) for c in lam_here]
            )
            total = total + y_now + y_prev(y_back)
            pair = (here, near[3, x, 1])
            chi_pair = [(near[j, x, 0], near[j, x, 1]) for j in range(3)]
            lam_pair = [(lam[j, x, 0], lam[j, x, 1]) for j in range(3)]
            beside = z_next(pair)
            chi_beside = [z_next(c) for c in chi_pair]
            lam_beside = [z_next(c) for c in lam_pair]
            z_now, z_back = zip(
                *[
                    face(
                        1,
                        pair[t],
                        beside[t],
                        [c[t] for c in chi_pair],
                        [c[t] for c in chi_beside],
                        [c[t] for c in lam_pair],
                        [c[t] for c in lam_beside],
                    )
                    for t in range(2)
                ]
            )
            gradient[x - 1] = total + z_now[0] + z_prev(z_back)[0]
        carried = back


def ring_steps(axis):
    count = lax.axis_size(axis)
    forward = [(i, (i + 1) % count) for i in range(count)]
    return forward, [(target, source) for source, target in forward]


def shards(labels, table, factor, chi, weights):
    layers, rows, columns = factor.shape
    assert rows == 8 and columns == 128 and layers % 2 == 0 and layers >= HALO
    peers = lax.axis_size("col") * lax.axis_size("slab")
    f32 = functools.partial(jax.ShapeDtypeStruct, dtype=jnp.float32)
    pairs = HALO // 2

    own, low_rows, high_rows, splat = pl.pallas_call(
        prepare,
        out_shape=(f32((4, layers, 8, 128)), f32((4, layers // 2, 8, 128)), f32((4, layers // 2, 8, 128)), f32((9, 8, 128))),
        in_specs=[HBM] * 5,
        out_specs=(VMEM,) * 4,
        scratch_shapes=[
            pltpu.VMEM((layers, 8, 128), jnp.int32),
            pltpu.SMEM((3,), jnp.float32),
            pltpu.VMEM((layers, 8, 128), jnp.float32),
            pltpu.SMEM((3, 3), jnp.float32),
            pltpu.SemaphoreType.DMA((5,)),
        ],
        compiler_params=PARAMS,
        name="prepare",
    )(labels, table, factor, chi, weights)

    forward, backward = ring_steps("slab")
    z_low = lax.ppermute(high_rows, "slab", forward)
    z_high = lax.ppermute(low_rows, "slab", backward)
    forward, backward = ring_steps("col")
    tail = layers // 2 - pairs
    x_low = lax.ppermute(
        jnp.concatenate([own[:, layers - HALO :], z_low[:, tail:], z_high[:, tail:]], axis=1), "col", forward
    )
    x_high = lax.ppermute(jnp.concatenate([own[:, :HALO], z_low[:, :pairs], z_high[:, :pairs]], axis=1), "col", backward)

    total = layers + 2 * HALO
    near, basis, sums = pl.pallas_call(
        functools.partial(krylov, layers, peers),
        out_shape=(f32((4, layers + 2, 2, 8, 128)), f32((3, 3, layers + 2, 2, 8, 128)), f32((peers, 128))),
        in_specs=[VMEM] * 6,
        out_specs=(VMEM,) * 3,
        scratch_shapes=[
            pltpu.VMEM((4, total, 8, 128), jnp.float32),
            pltpu.VMEM((3, total, 2, 8, 128), jnp.float32),
            pltpu.VMEM((3, 3, total, 2, 8, 128), jnp.float32),
        ],
        compiler_params=PARAMS,
        name="krylov",
    )(own, z_low, z_high, x_low, x_high, splat)

    gathered = lax.all_to_all(sums, ("col", "slab"), 0, 0, tiled=True)

    return pl.pallas_call(
        functools.partial(finish, layers),
        out_shape=(f32((3, layers, 8, 128)), f32((layers, 8, 128))),
        in_specs=[VMEM] * 4,
        out_specs=(VMEM,) * 2,
        scratch_shapes=[pltpu.VMEM((3, layers + 2, 2, 8, 128), jnp.float32)],
        compiler_params=PARAMS,
        name="finish",
    )(gathered, near, basis, splat)


def solution(mesh):
    in_specs = (
        P("col", "slab", None),
        P(),
        P("col", "slab", None),
        P(None, "col", "slab", None),
        P(),
    )
    out_specs = (P(None, "col", "slab", None), P("col", "slab", None))
    return jax.shard_map(shards, mesh=mesh, in_specs=in_specs, out_specs=out_specs, check_vma=False)
```

```python
import functools

import jax
import jax.numpy as jnp
from jax import lax
from jax.experimental import pallas as pl
from jax.experimental.pallas import tpu as pltpu
from jax.sharding import PartitionSpec as P


mass_shift = 0.01
HALO = 4
MOMENTS = 6

VMEM = pl.BlockSpec(memory_space=pltpu.VMEM)
HBM = pl.BlockSpec(memory_space=pltpu.HBM)
PARAMS = pltpu.CompilerParams(vmem_limit_bytes=8 * 2**20)


def tile_iota(axis):
    return lax.broadcasted_iota(jnp.int32, (8, 128), axis)


def y_next(tile):
    return pltpu.roll(tile, 127, 1)


def y_prev(tile):
    return pltpu.roll(tile, 1, 1)


def z_next(pair):
    last = tile_iota(0) == 7
    first, second = (pltpu.roll(tile, 7, 0) for tile in pair)
    return jnp.where(last, second, first), jnp.where(last, first, second)


def z_prev(pair):
    top = tile_iota(0) == 0
    first, second = (pltpu.roll(tile, 1, 0) for tile in pair)
    return jnp.where(top, second, first), jnp.where(top, first, second)


def prepare(
    labels_hbm, table_hbm, factor_hbm, chi_hbm, weights_hbm, own_low, own_high, low_rows, high_rows, splat,
    labels, table, factor, weights, sems,
):
    moves = (
        (labels_hbm, labels),
        (table_hbm, table),
        (factor_hbm, factor),
        (chi_hbm.at[:, pl.ds(0, HALO)], own_low.at[pl.ds(0, 3)]),
        (chi_hbm.at[:, pl.ds(HALO, HALO)], own_high.at[pl.ds(0, 3)]),
        (weights_hbm, weights),
    )
    copies = [pltpu.make_async_copy(source, target, sems.at[n]) for n, (source, target) in enumerate(moves)]
    for copy in copies:
        copy.start()
    for copy in copies:
        copy.wait()
    for x in range(2 * HALO):
        label = labels[x]
        block = own_low if x < HALO else own_high
        block[3, x % HALO] = jnp.where(label == 0, table[0], jnp.where(label == 1, table[1], table[2])) * factor[x]
    for i in range(3):
        for j in range(3):
            splat[3 * i + j] = jnp.full((8, 128), weights[i, j], jnp.float32)
    half = tile_iota(0) < 4
    for f in range(4):
        for i in range(HALO):
            block = own_low if 2 * i < HALO else own_high
            even, odd = block[f, 2 * i % HALO], block[f, (2 * i + 1) % HALO]
            low_rows[f, i] = jnp.where(half, even, pltpu.roll(odd, 4, 0))
            high_rows[f, i] = jnp.where(half, pltpu.roll(even, 4, 0), odd)


def fold(z_low, z_high, ring, low_corner, high_corner):
    half = tile_iota(0) < 4
    for f in range(4):
        tiles = []
        for i in range(HALO):
            up, down = z_high[f, i], z_low[f, i]
            tiles.append(jnp.where(half, up, pltpu.roll(down, 4, 0)))
            tiles.append(jnp.where(half, pltpu.roll(up, 4, 0), down))
        for x, tile in enumerate(tiles):
            ring[f, x] = tile
        outer = (tile_iota(0) < 2) | (tile_iota(0) >= 6)
        for corner, (first, second, third) in ((low_corner, tiles[:3]), (high_corner, tiles[:-4:-1])):
            corner[f, 0] = first
            corner[f, 1] = jnp.where(outer, second, jnp.where(half, pltpu.roll(third, 2, 0), pltpu.roll(third, 6, 0)))


def two_sum(a, b):
    total = a + b
    part = total - a
    return total, (a - (total - part)) + (b - part)


def two_product(a, b):
    product = a * b
    a_top, b_top = [4097.0 * v - (4097.0 * v - v) for v in (a, b)]
    a_rest, b_rest = a - a_top, b - b_top
    return product, ((a_top * b_top - product) + a_top * b_rest + a_rest * b_top) + a_rest * b_rest


def pair_sum(a, b):
    total, error = two_sum(a[0], b[0])
    return total, error + (a[1] + b[1])


def pair_product(a, b):
    product, error = two_product(a[0], b[0])
    return product, error + (a[0] * b[1] + a[1] * b[0])


def total_row(tiles):
    row = tile_iota(0)
    lane = tile_iota(1)
    pairs = [(tile, jnp.zeros((8, 128), jnp.float32)) for tile in tiles]
    place = [[n] for n in range(len(tiles))]
    for width in (4, 2, 1):
        lower = (row & width) == 0
        merged, spots = [], []
        for n in range(0, len(pairs), 2):
            first, second = pairs[n], pairs[min(n + 1, len(pairs) - 1)]
            kept = [jnp.where(lower, a, b) for a, b in zip(first, second)]
            moved = [jnp.where(lower, pltpu.roll(a, 8 - width, 0), pltpu.roll(b, width, 0)) for a, b in zip(first, second)]
            merged.append(pair_sum(kept, moved))
            spots.append((place[n], place[n + 1] if n + 1 < len(pairs) else None))
        pairs, place = merged, spots
    result = jnp.zeros((8, 128), jnp.float32)

    def home(spot, at, width):
        if spot is None:
            return
        if len(spot) == 1:
            yield spot[0], at
            return
        yield from home(spot[0], at, 2 * width)
        yield from home(spot[1], at + width, 2 * width)

    for pair, spot in zip(pairs, place):
        for shift in (64, 32, 16, 8, 4, 2, 1):
            pair = pair_sum(pair, [pltpu.roll(a, shift, 1) for a in pair])
        for n, at in home(spot, 0, 1):
            result = jnp.where((row == at) & (lane == 4 * n), pair[0], result)
            result = jnp.where((row == at) & (lane == 4 * n + 1), pair[1], result)
    return jnp.sum(result, axis=0, keepdims=True)


def krylov(peers, own_low, own_high, z_ring, x_low, x_high, corner_low, corner_high, splat, near, basis, sums, ring, cond, field):
    layers = 2 * HALO
    total = 2 * layers
    half = tile_iota(0) < 4

    for f in range(4):
        for corner, spots in ((corner_low, (3, 2, 1, 0)), (corner_high, (12, 13, 14, 15))):
            shared = corner[f, 1]
            ring[f, spots[0]] = corner[f, 0]
            ring[f, spots[1]] = shared
            third = jnp.where(half, pltpu.roll(shared, 6, 0), pltpu.roll(shared, 2, 0))
            ring[f, spots[2]] = third
            ring[f, spots[3]] = third

    def grid(f, x):
        block = (x_low, own_low, own_high, x_high)[x // HALO]
        inside = HALO <= x < HALO + layers
        return block[f, x % HALO], z_ring[f, x - HALO] if inside else ring[f, x]

    def harmonic(here, after):
        return 2.0 * here * after / (here + after)

    for x in range(total - 1):
        here = grid(3, x)
        after = grid(3, x + 1)
        beside = z_next(here)
        for t in range(2):
            cond[0, x, t] = harmonic(here[t], after[t])
            cond[1, x, t] = harmonic(here[t], beside[t])
            cond[2, x, t] = harmonic(here[t], y_next(here[t]))

    def out_flow(x, here, after, offset, flows):
        beside = z_next(here)
        added = []
        z_flux = []
        for t in range(2):
            z_flux.append(cond[1, x, t] * (offset[1] + (beside[t] - here[t])))
        z_back = z_prev(z_flux)
        for t in range(2):
            x_flux = cond[0, x, t] * (offset[0] + (after[t] - here[t]))
            y_flux = cond[2, x, t] * (offset[2] + (y_next(here[t]) - here[t]))
            before = flows[t]
            flows[t] = x_flux
            if before is not None:
                added.append((before - x_flux) + (z_back[t] - z_flux[t]) + (y_prev(y_flux) - y_flux))
        return added

    flows = [[None, None] for _ in range(3)]
    for j in range(3):
        for t in range(2):
            here, after = grid(j, 0)[t], grid(j, 1)[t]
            flows[j][t] = cond[0, 0, t] * ((1.0 if j == 0 else 0.0) + (after - here))
    for x in range(1, total - 1):
        drive = []
        for j in range(3):
            offset = [1.0 if d == j else 0.0 for d in range(3)]
            drive.append(out_flow(x, grid(j, x), grid(j, x + 1), offset, flows[j]))
        for i in range(3):
            for t in range(2):
                field[0, i, x, t] = (
                    splat[3 * i] * drive[0][t] + splat[3 * i + 1] * drive[1][t] + splat[3 * i + 2] * drive[2][t]
                )

    for k in (1, 2):
        for i in range(3):
            first = k
            flow = [cond[0, first, t] * (field[k - 1, i, first + 1, t] - field[k - 1, i, first, t]) for t in range(2)]
            for x in range(first + 1, total - 1 - k):
                here = (field[k - 1, i, x, 0], field[k - 1, i, x, 1])
                after = (field[k - 1, i, x + 1, 0], field[k - 1, i, x + 1, 1])
                added = out_flow(x, here, after, (0.0, 0.0, 0.0), flow)
                for t in range(2):
                    field[k, i, x, t] = mass_shift * here[t] + added[t]

    partial = [jnp.zeros((8, 128), jnp.float32) for _ in range(3 * MOMENTS)]
    for i in range(3):
        flow = [cond[0, HALO - 1, 0] * (field[2, i, HALO, 0] - field[2, i, HALO - 1, 0]), jnp.zeros((8, 128), jnp.float32)]
        for x in range(HALO, HALO + layers):
            here = (field[2, i, x, 0], field[2, i, x, 1])
            after = (field[2, i, x + 1, 0], field[2, i, x + 1, 1])
            added = out_flow(x, here, after, (0.0, 0.0, 0.0), flow)
            v = [field[0, i, x, 0], field[1, i, x, 0], here[0], mass_shift * here[0] + added[0]]
            for m, (a, b) in enumerate(((0, 0), (0, 1), (1, 1), (1, 2), (2, 2), (2, 3))):
                partial[3 * m + i] = partial[3 * m + i] + v[a] * v[b]
    sums[...] = jnp.broadcast_to(total_row(partial), (peers, 128))

    for x in range(layers + 2):
        for t in range(2):
            for f in range(4):
                near[f, x, t] = grid(f, x + HALO - 1)[t]
            for k in range(3):
                for i in range(3):
                    basis[k, i, x, t] = field[k, i, x + HALO - 1, t]


def quadratic(terms):
    products = [pair_product(a, b) for a, b in terms]
    total = products[0]
    for product in products[1:]:
        total = pair_sum(total, product)
    return total[0] + total[1]


def coefficients(sums):
    count = sums.shape[0] // 8
    pairs = [(sums[8 * n : 8 * n + 8], jnp.zeros((8, 128), jnp.float32)) for n in range(count)]
    while len(pairs) > 1:
        tail = pairs[len(pairs) // 2 * 2 :]
        pairs = [pair_sum(pairs[n], pairs[n + 1]) for n in range(0, len(pairs) - 1, 2)] + tail
    pair = pairs[0]
    for shift in (4, 2, 1):
        pair = pair_sum(pair, [pltpu.roll(a, shift, 0) for a in pair])
    value, error = pair[0], pair[1] + pltpu.roll(pair[0], 127, 1)

    def moment(m):
        if m == 0:
            return value, error
        return pltpu.roll(value, 128 - 12 * m, 1), pltpu.roll(error, 128 - 12 * m, 1)

    m0, m1, m2, m3, m4, m5 = [moment(m) for m in range(MOMENTS)]
    none = jnp.zeros((8, 128), jnp.float32)
    one = (jnp.ones((8, 128), jnp.float32), none)
    alpha0 = m0[0] / m1[0]
    alpha0_squared = two_product(alpha0, alpha0)
    norm1 = quadratic(((one, m0), ((-2.0 * alpha0, none), m1), (alpha0_squared, m2)))
    grow = 1.0 + norm1 / m0[0]
    curve1 = quadratic(
        ((two_product(grow, grow), m1), (two_product(-2.0 * grow, alpha0), m2), (alpha0_squared, m3))
    )
    alpha1 = norm1 / curve1
    r1 = -(alpha0 + alpha1 * grow)
    r2 = alpha1 * alpha0
    norm2 = quadratic(
        (
            (one, m0),
            ((2.0 * r1, none), m1),
            (pair_sum(two_product(r1, r1), (2.0 * r2, none)), m2),
            (two_product(2.0 * r1, r2), m3),
            (two_product(r2, r2), m4),
        )
    )
    beta1 = norm2 / norm1
    p0, p1, p2 = 1.0 + beta1 * grow, r1 - beta1 * alpha0, r2
    curve2 = quadratic(
        (
            (two_product(p0, p0), m1),
            (two_product(2.0 * p0, p1), m2),
            (pair_sum(two_product(p1, p1), two_product(2.0 * p0, p2)), m3),
            (two_product(2.0 * p1, p2), m4),
            (two_product(p2, p2), m5),
        )
    )
    alpha2 = norm2 / curve2
    return alpha0 + alpha1 * grow + alpha2 * p0, alpha2 * p1 - alpha1 * alpha0, alpha2 * p2


def finish(sums, near, basis, splat, adjoint_hbm, gradient_hbm, adjoint, gradient, lam, sems):
    layers = 2 * HALO
    lane = tile_iota(1)
    copies = []
    scale = []
    for c in coefficients(sums):
        scale.append([jnp.sum(jnp.where(lane == 4 * i, c, 0.0), axis=1, keepdims=True) for i in range(3)])
    for i in range(3):
        for x in range(layers + 2):
            for t in range(2):
                if t == 1 and x in (0, layers + 1):
                    continue
                value = scale[0][i] * basis[0, i, x, t] + scale[1][i] * basis[1, i, x, t] + scale[2][i] * basis[2, i, x, t]
                lam[i, x, t] = value
                if t == 0 and 0 < x <= layers:
                    adjoint[i, x - 1] = value
        copies.append(pltpu.make_async_copy(adjoint.at[i], adjoint_hbm.at[i], sems.at[i]))
        copies[-1].start()

    def face(d, here, after, chi_here, chi_after, lam_here, lam_after):
        local = [(1.0 if j == d else 0.0) + (chi_after[j] - chi_here[j]) for j in range(3)]
        h_term = None
        for i in range(3):
            inner = splat[3 * i] * local[0] + splat[3 * i + 1] * local[1] + splat[3 * i + 2] * local[2]
            part = local[i] * (inner - (lam_after[i] - lam_here[i]))
            h_term = part if h_term is None else h_term + part
        inverse = 1.0 / (here + after)
        share = after * inverse
        rest = here * inverse
        return h_term * (2.0 * share * share), h_term * (2.0 * rest * rest)

    carried = None
    for x in range(layers + 1):
        now, back = face(
            0,
            near[3, x, 0],
            near[3, x + 1, 0],
            [near[j, x, 0] for j in range(3)],
            [near[j, x + 1, 0] for j in range(3)],
            [lam[j, x, 0] for j in range(3)],
            [lam[j, x + 1, 0] for j in range(3)],
        )
        if x > 0:
            total = now + carried
            here = near[3, x, 0]
            chi_here = [near[j, x, 0] for j in range(3)]
            lam_here = [lam[j, x, 0] for j in range(3)]
            y_now, y_back = face(
                2, here, y_next(here), chi_here, [y_next(c) for c in chi_here], lam_here, [y_next(c) for c in lam_here]
            )
            total = total + y_now + y_prev(y_back)
            pair = (here, near[3, x, 1])
            chi_pair = [(near[j, x, 0], near[j, x, 1]) for j in range(3)]
            lam_pair = [(lam[j, x, 0], lam[j, x, 1]) for j in range(3)]
            beside = z_next(pair)
            chi_beside = [z_next(c) for c in chi_pair]
            lam_beside = [z_next(c) for c in lam_pair]
            z_now, z_back = zip(
                *[
                    face(
                        1,
                        pair[t],
                        beside[t],
                        [c[t] for c in chi_pair],
                        [c[t] for c in chi_beside],
                        [c[t] for c in lam_pair],
                        [c[t] for c in lam_beside],
                    )
                    for t in range(2)
                ]
            )
            gradient[x - 1] = total + z_now[0] + z_prev(z_back)[0]
            if x % HALO == 0:
                part = pl.ds(x - HALO, HALO)
                copies.append(pltpu.make_async_copy(gradient.at[part], gradient_hbm.at[part], sems.at[2 + x // HALO]))
                copies[-1].start()
        carried = back
    for copy in copies:
        copy.wait()


def ring_steps(axis):
    count = lax.axis_size(axis)
    forward = [(i, (i + 1) % count) for i in range(count)]
    return forward, [(target, source) for source, target in forward]


def in_hbm(*arrays):
    return [pltpu.with_memory_space_constraint(a, pltpu.HBM) for a in arrays]


def shards(labels, table, factor, chi, weights):
    layers = factor.shape[0]
    assert factor.shape == (2 * HALO, 8, 128)
    peers = lax.axis_size("col") * lax.axis_size("slab")
    f32 = functools.partial(jax.ShapeDtypeStruct, dtype=jnp.float32)
    scratch = functools.partial(pltpu.VMEM, dtype=jnp.float32)
    half_block = f32((4, HALO, 8, 128))

    own_low, own_high, low_rows, high_rows, splat = pl.pallas_call(
        prepare,
        out_shape=(half_block,) * 4 + (f32((9, 8, 128)),),
        in_specs=[HBM] * 5,
        out_specs=(VMEM,) * 5,
        scratch_shapes=[
            pltpu.VMEM((layers, 8, 128), jnp.int32),
            pltpu.SMEM((3,), jnp.float32),
            scratch((layers, 8, 128)),
            pltpu.SMEM((3, 3), jnp.float32),
            pltpu.SemaphoreType.DMA((6,)),
        ],
        compiler_params=PARAMS,
        name="prepare",
    )(*in_hbm(labels, table, factor, chi, weights))

    forward, backward = ring_steps("slab")
    z_low = lax.ppermute(high_rows, "slab", forward)
    z_high = lax.ppermute(low_rows, "slab", backward)
    forward, backward = ring_steps("col")
    x_low = lax.ppermute(own_high, "col", forward)
    x_high = lax.ppermute(own_low, "col", backward)

    ring, low_corner, high_corner = pl.pallas_call(
        fold,
        out_shape=(f32((4, layers, 8, 128)), f32((4, 2, 8, 128)), f32((4, 2, 8, 128))),
        in_specs=[VMEM] * 2,
        out_specs=(VMEM,) * 3,
        compiler_params=PARAMS,
        name="fold",
    )(z_low, z_high)
    corner_low = lax.ppermute(high_corner, "col", forward)
    corner_high = lax.ppermute(low_corner, "col", backward)

    near, basis, sums = pl.pallas_call(
        functools.partial(krylov, peers),
        out_shape=(f32((4, layers + 2, 2, 8, 128)), f32((3, 3, layers + 2, 2, 8, 128)), f32((peers, 128))),
        in_specs=[VMEM] * 8,
        out_specs=(VMEM,) * 3,
        scratch_shapes=[
            scratch((4, 2 * layers, 8, 128)),
            scratch((3, 2 * layers, 2, 8, 128)),
            scratch((3, 3, 2 * layers, 2, 8, 128)),
        ],
        compiler_params=PARAMS,
        name="krylov",
    )(own_low, own_high, ring, x_low, x_high, corner_low, corner_high, splat)

    gathered = lax.all_to_all(sums, ("col", "slab"), 0, 0, tiled=True)

    return pl.pallas_call(
        finish,
        out_shape=(f32((3, layers, 8, 128)), f32((layers, 8, 128))),
        in_specs=[VMEM] * 4,
        out_specs=(HBM,) * 2,
        scratch_shapes=[
            scratch((3, layers, 8, 128)),
            scratch((layers, 8, 128)),
            scratch((3, layers + 2, 2, 8, 128)),
            pltpu.SemaphoreType.DMA((5,)),
        ],
        compiler_params=PARAMS,
        name="finish",
    )(gathered, near, basis, splat)


def solution(mesh):
    in_specs = (
        P("col", "slab", None),
        P(),
        P("col", "slab", None),
        P(None, "col", "slab", None),
        P(),
    )
    out_specs = (P(None, "col", "slab", None), P("col", "slab", None))
    return jax.shard_map(shards, mesh=mesh, in_specs=in_specs, out_specs=out_specs, check_vma=False)
```

```python
import functools

import jax
import jax.numpy as jnp
from jax import lax
from jax.experimental import pallas as pl
from jax.experimental.pallas import tpu as pltpu
from jax.sharding import PartitionSpec as P


mass_shift = 0.01
HALO = 4
MOMENTS = 6

VMEM = pl.BlockSpec(memory_space=pltpu.VMEM)
HBM = pl.BlockSpec(memory_space=pltpu.HBM)
PARAMS = pltpu.CompilerParams(vmem_limit_bytes=8 * 2**20)


def tile_iota(axis):
    return lax.broadcasted_iota(jnp.int32, (8, 128), axis)


def y_next(tile):
    return pltpu.roll(tile, 127, 1)


def y_prev(tile):
    return pltpu.roll(tile, 1, 1)


def z_next(pair):
    last = tile_iota(0) == 7
    first, second = (pltpu.roll(tile, 7, 0) for tile in pair)
    return jnp.where(last, second, first), jnp.where(last, first, second)


def z_prev(pair):
    top = tile_iota(0) == 0
    first, second = (pltpu.roll(tile, 1, 0) for tile in pair)
    return jnp.where(top, second, first), jnp.where(top, first, second)


def parity(axis):
    return lax.rem(lax.axis_index(axis), 2)


def choose(odd, if_even, if_odd):
    return jnp.where(jnp.full((8, 128), odd, jnp.int32) == 0, if_even, if_odd)


def prepare(
    labels_hbm, table_hbm, factor_hbm, chi_hbm, weights_hbm, own, x_a, x_b, z_a, z_b, splat,
    labels, table, factor, weights, sems,
):
    odd_col = parity("col")
    start_a, start_b = HALO * (1 - odd_col), HALO * odd_col
    moves = (
        (labels_hbm, labels),
        (table_hbm, table),
        (factor_hbm, factor),
        (weights_hbm, weights),
        (chi_hbm, own.at[pl.ds(0, 3)]),
        (chi_hbm.at[:, pl.ds(start_a, HALO)], x_a.at[pl.ds(0, 3)]),
        (chi_hbm.at[:, pl.ds(start_b, HALO)], x_b.at[pl.ds(0, 3)]),
    )
    copies = [pltpu.make_async_copy(source, target, sems.at[n]) for n, (source, target) in enumerate(moves)]
    for copy in copies:
        copy.start()
    for copy in copies:
        copy.wait()
    for x in range(2 * HALO):
        label = labels[x]
        own[3, x] = jnp.where(label == 0, table[0], jnp.where(label == 1, table[1], table[2])) * factor[x]
    for x in range(HALO):
        low, high = own[3, x], own[3, HALO + x]
        x_a[3, x] = choose(odd_col, high, low)
        x_b[3, x] = choose(odd_col, low, high)
    for i in range(3):
        for j in range(3):
            splat[3 * i + j] = jnp.full((8, 128), weights[i, j], jnp.float32)
    odd_slab = parity("slab")
    half = tile_iota(0) < 4
    for f in range(4):
        for i in range(HALO):
            even, odd = own[f, 2 * i], own[f, 2 * i + 1]
            low_rows = jnp.where(half, even, pltpu.roll(odd, 4, 0))
            high_rows = jnp.where(half, pltpu.roll(even, 4, 0), odd)
            z_a[f, i] = choose(odd_slab, high_rows, low_rows)
            z_b[f, i] = choose(odd_slab, low_rows, high_rows)


def fold(z_a, z_b, ring, corner_a, corner_b):
    odd_col, odd_slab = parity("col"), parity("slab")
    half = tile_iota(0) < 4
    outer = (tile_iota(0) < 2) | (tile_iota(0) >= 6)

    def packed(first, second, third):
        return first, jnp.where(outer, second, jnp.where(half, pltpu.roll(third, 2, 0), pltpu.roll(third, 6, 0)))

    for f in range(4):
        tiles = []
        for i in range(HALO):
            up, down = choose(odd_slab, z_a[f, i], z_b[f, i]), choose(odd_slab, z_b[f, i], z_a[f, i])
            tiles.append(jnp.where(half, up, pltpu.roll(down, 4, 0)))
            tiles.append(jnp.where(half, pltpu.roll(up, 4, 0), down))
        for x, tile in enumerate(tiles):
            ring[f, x] = tile
        for n, (low, high) in enumerate(zip(packed(*tiles[:3]), packed(*tiles[:-4:-1]))):
            corner_a[f, n] = choose(odd_col, high, low)
            corner_b[f, n] = choose(odd_col, low, high)


def two_sum(a, b):
    total = a + b
    part = total - a
    return total, (a - (total - part)) + (b - part)


def two_product(a, b):
    product = a * b
    a_top, b_top = [4097.0 * v - (4097.0 * v - v) for v in (a, b)]
    a_rest, b_rest = a - a_top, b - b_top
    return product, ((a_top * b_top - product) + a_top * b_rest + a_rest * b_top) + a_rest * b_rest


def pair_sum(a, b):
    total, error = two_sum(a[0], b[0])
    return total, error + (a[1] + b[1])


def pair_product(a, b):
    product, error = two_product(a[0], b[0])
    return product, error + (a[0] * b[1] + a[1] * b[0])


def total_row(tiles):
    row = tile_iota(0)
    lane = tile_iota(1)
    pairs = [(tile, jnp.zeros((8, 128), jnp.float32)) for tile in tiles]
    place = [[n] for n in range(len(tiles))]
    for width in (4, 2, 1):
        lower = (row & width) == 0
        merged, spots = [], []
        for n in range(0, len(pairs), 2):
            first, second = pairs[n], pairs[min(n + 1, len(pairs) - 1)]
            kept = [jnp.where(lower, a, b) for a, b in zip(first, second)]
            moved = [jnp.where(lower, pltpu.roll(a, 8 - width, 0), pltpu.roll(b, width, 0)) for a, b in zip(first, second)]
            merged.append(pair_sum(kept, moved))
            spots.append((place[n], place[n + 1] if n + 1 < len(pairs) else None))
        pairs, place = merged, spots
    result = jnp.zeros((8, 128), jnp.float32)

    def home(spot, at, width):
        if spot is None:
            return
        if len(spot) == 1:
            yield spot[0], at
            return
        yield from home(spot[0], at, 2 * width)
        yield from home(spot[1], at + width, 2 * width)

    for pair, spot in zip(pairs, place):
        for shift in (64, 32, 16, 8, 4, 2, 1):
            pair = pair_sum(pair, [pltpu.roll(a, shift, 1) for a in pair])
        for n, at in home(spot, 0, 1):
            result = jnp.where((row == at) & (lane == 4 * n), pair[0], result)
            result = jnp.where((row == at) & (lane == 4 * n + 1), pair[1], result)
    return jnp.sum(result, axis=0, keepdims=True)


LAYERS = 2 * HALO
TOTAL = 2 * LAYERS


def inner(k):
    return range(HALO + 1 + k, HALO + LAYERS - 1 - k)


def harmonic(here, after):
    return 2.0 * here * after / (here + after)


def out_flow(here, after, x_cond, z_cond, y_cond, offset, flows):
    beside = z_next(here)
    z_flux = [z_cond[t] * (offset[1] + (beside[t] - here[t])) for t in range(2)]
    z_back = z_prev(z_flux)
    added = []
    for t in range(2):
        x_flux = x_cond[t] * (offset[0] + (after[t] - here[t]))
        y_flux = y_cond[t] * (offset[2] + (y_next(here[t]) - here[t]))
        before = flows[t]
        flows[t] = x_flux
        added.append((before - x_flux) + (z_back[t] - z_flux[t]) + (y_prev(y_flux) - y_flux))
    return added


def both(read, *index):
    return [read(*index, t) for t in range(2)]


def add_source(layers, grid, cond, splat, field):
    offset = [[1.0 if d == j else 0.0 for d in range(3)] for j in range(3)]
    flows = []
    for j in range(3):
        here, after = both(grid, j, layers[0] - 1), both(grid, j, layers[0])
        flows.append([cond(0, layers[0] - 1, t) * (offset[j][0] + (after[t] - here[t])) for t in range(2)])
    for x in layers:
        conds = [both(cond, d, x) for d in range(3)]
        drive = [
            out_flow(both(grid, j, x), both(grid, j, x + 1), *conds, offset[j], flows[j]) for j in range(3)
        ]
        for i in range(3):
            for t in range(2):
                field[0, i, x, t] = (
                    splat[3 * i] * drive[0][t] + splat[3 * i + 1] * drive[1][t] + splat[3 * i + 2] * drive[2][t]
                )


def applied(k, i, layers, v, cond):
    here, after = both(v, k, i, layers[0] - 1), both(v, k, i, layers[0])
    flow = [cond(0, layers[0] - 1, t) * (after[t] - here[t]) for t in range(2)]
    for x in layers:
        here, after = both(v, k, i, x), both(v, k, i, x + 1)
        added = out_flow(here, after, *[both(cond, d, x) for d in range(3)], (0.0, 0.0, 0.0), flow)
        yield x, [mass_shift * here[t] + added[t] for t in range(2)]


def face_parts(d, here, after, chi_here, chi_after, splat):
    local = [(1.0 if j == d else 0.0) + (chi_after[j] - chi_here[j]) for j in range(3)]
    energy = None
    for i in range(3):
        part = local[i] * (splat[3 * i] * local[0] + splat[3 * i + 1] * local[1] + splat[3 * i + 2] * local[2])
        energy = part if energy is None else energy + part
    inverse = 1.0 / (here + after)
    share = after * inverse
    rest = here * inverse
    now, back = 2.0 * share * share, 2.0 * rest * rest
    return [energy * now] + [value * now for value in local], [energy * back] + [value * back for value in local]


def early(own, ring, x_a, x_b, splat, halo, cond, field, base, slopes):
    odd_col = parity("col")
    for f in range(4):
        for n in range(HALO):
            halo[f, n] = choose(odd_col, x_b[f, n], x_a[f, n])
            halo[f, HALO + n] = choose(odd_col, x_a[f, n], x_b[f, n])

    def grid(f, x, t):
        if t == 1:
            return ring[f, x - HALO]
        if x < HALO:
            return halo[f, x]
        return own[f, x - HALO] if x < HALO + LAYERS else halo[f, x - LAYERS]

    for x in range(TOTAL):
        here = grid(3, x, 0)
        cond[2, x, 0] = harmonic(here, y_next(here))
        if x + 1 < TOTAL:
            cond[0, x, 0] = harmonic(here, grid(3, x + 1, 0))
        if HALO <= x < HALO + LAYERS:
            other = grid(3, x, 1)
            cond[2, x, 1] = harmonic(other, y_next(other))
            if x + 1 < HALO + LAYERS:
                cond[0, x, 1] = harmonic(other, grid(3, x + 1, 1))
            for t, (tile, beside) in enumerate(zip((here, other), z_next((here, other)))):
                cond[1, x, t] = harmonic(tile, beside)

    def ready(*index):
        return cond[index]

    def v(*index):
        return field[index]

    add_source(inner(0), grid, ready, splat, field)
    for k in (1, 2):
        for i in range(3):
            for x, value in applied(k - 1, i, inner(k), v, ready):
                field[k, i, x, 0], field[k, i, x, 1] = value

    carried = None
    for x in range(HALO - 1, HALO + LAYERS):
        here, after = [[grid(f, n, 0) for f in range(4)] for n in (x, x + 1)]
        now, back = face_parts(0, here[3], after[3], here[:3], after[:3], splat)
        if carried is not None:
            beside = [y_next(tile) for tile in here]
            y_now, y_back = face_parts(2, here[3], beside[3], here[:3], beside[:3], splat)
            y_back = [y_prev(tile) for tile in y_back]
            pairs = [(here[f], grid(f, x, 1)) for f in range(4)]
            nexts = [z_next(pair) for pair in pairs]
            z_now, z_back = zip(
                *[
                    face_parts(1, pairs[3][t], nexts[3][t], [p[t] for p in pairs[:3]], [p[t] for p in nexts[:3]], splat)
                    for t in range(2)
                ]
            )
            z_now, z_back = z_now[0], [z_prev(pair)[0] for pair in zip(*z_back)]
            sides = ((now, carried), (z_now, z_back), (y_now, y_back))
            base[x - HALO] = sum(side[0] for pair in sides for side in pair)
            for d in range(3):
                for n in range(2):
                    for j in range(3):
                        slopes[d, n, j, x - HALO] = sides[d][n][1 + j]
        carried = back


def krylov(peers, own, z_ring, halo, corner_a, corner_b, splat, early_cond, early_field, field, sums, ring, cond):
    odd_col = parity("col")
    half = tile_iota(0) < 4
    for f in range(4):
        tiles = [(corner_a[f, n], corner_b[f, n]) for n in range(2)]
        low = [choose(odd_col, b, a) for a, b in tiles]
        high = [choose(odd_col, a, b) for a, b in tiles]
        for (first, shared), spots in ((low, (3, 2, 1, 0)), (high, (4, 5, 6, 7))):
            third = jnp.where(half, pltpu.roll(shared, 6, 0), pltpu.roll(shared, 2, 0))
            for spot, tile in zip(spots, (first, shared, third, third)):
                ring[f, spot] = tile

    def grid(f, x, t):
        if x < HALO:
            return (halo, ring)[t][f, x]
        if x < HALO + LAYERS:
            return (own, z_ring)[t][f, x - HALO]
        return (halo, ring)[t][f, x - LAYERS]

    def is_early(d, x, t):
        return HALO <= x < HALO + LAYERS - (1 if d == 0 and t == 1 else 0) or (t == 0 and d != 1)

    def ready(d, x, t):
        return (early_cond if is_early(d, x, t) else cond)[d, x, t]

    def v(k, i, x, t):
        return (early_field if x in inner(k) else field)[k, i, x, t]

    for x in range(TOTAL - 1):
        here = both(grid, 3, x)
        if not is_early(0, x, 1):
            cond[0, x, 1] = harmonic(here[1], grid(3, x + 1, 1))
        if not is_early(2, x, 1):
            cond[2, x, 1] = harmonic(here[1], y_next(here[1]))
        if not is_early(1, x, 1):
            for t, beside in enumerate(z_next(here)):
                cond[1, x, t] = harmonic(here[t], beside)

    def outer(k):
        done = inner(k)
        return range(1 + k, done.start), range(done.stop, TOTAL - 1 - k)

    for layers in outer(0):
        add_source(layers, grid, ready, splat, field)
    for k in (1, 2):
        for layers in outer(k):
            for i in range(3):
                for x, value in applied(k - 1, i, layers, v, ready):
                    field[k, i, x, 0], field[k, i, x, 1] = value

    partial = [jnp.zeros((8, 128), jnp.float32) for _ in range(3 * MOMENTS)]
    for i in range(3):
        for x, value in applied(2, i, range(HALO, HALO + LAYERS), v, ready):
            tiles = [v(k, i, x, 0) for k in range(3)] + [value[0]]
            for m, (a, b) in enumerate(((0, 0), (0, 1), (1, 1), (1, 2), (2, 2), (2, 3))):
                partial[3 * m + i] = partial[3 * m + i] + tiles[a] * tiles[b]
    sums[...] = jnp.broadcast_to(total_row(partial), (peers, 128))


def quadratic(terms):
    products = [pair_product(a, b) for a, b in terms]
    total = products[0]
    for product in products[1:]:
        total = pair_sum(total, product)
    return total[0] + total[1]


def coefficients(sums):
    count = sums.shape[0] // 8
    pairs = [(sums[8 * n : 8 * n + 8], jnp.zeros((8, 128), jnp.float32)) for n in range(count)]
    while len(pairs) > 1:
        tail = pairs[len(pairs) // 2 * 2 :]
        pairs = [pair_sum(pairs[n], pairs[n + 1]) for n in range(0, len(pairs) - 1, 2)] + tail
    pair = pairs[0]
    for shift in (4, 2, 1):
        pair = pair_sum(pair, [pltpu.roll(a, shift, 0) for a in pair])
    value, error = pair[0], pair[1] + pltpu.roll(pair[0], 127, 1)

    def moment(m):
        if m == 0:
            return value, error
        return pltpu.roll(value, 128 - 12 * m, 1), pltpu.roll(error, 128 - 12 * m, 1)

    m0, m1, m2, m3, m4, m5 = [moment(m) for m in range(MOMENTS)]
    none = jnp.zeros((8, 128), jnp.float32)
    one = (jnp.ones((8, 128), jnp.float32), none)
    alpha0 = m0[0] / m1[0]
    alpha0_squared = two_product(alpha0, alpha0)
    norm1 = quadratic(((one, m0), ((-2.0 * alpha0, none), m1), (alpha0_squared, m2)))
    grow = 1.0 + norm1 / m0[0]
    curve1 = quadratic(
        ((two_product(grow, grow), m1), (two_product(-2.0 * grow, alpha0), m2), (alpha0_squared, m3))
    )
    alpha1 = norm1 / curve1
    r1 = -(alpha0 + alpha1 * grow)
    r2 = alpha1 * alpha0
    norm2 = quadratic(
        (
            (one, m0),
            ((2.0 * r1, none), m1),
            (pair_sum(two_product(r1, r1), (2.0 * r2, none)), m2),
            (two_product(2.0 * r1, r2), m3),
            (two_product(r2, r2), m4),
        )
    )
    beta1 = norm2 / norm1
    p0, p1, p2 = 1.0 + beta1 * grow, r1 - beta1 * alpha0, r2
    curve2 = quadratic(
        (
            (two_product(p0, p0), m1),
            (two_product(2.0 * p0, p1), m2),
            (pair_sum(two_product(p1, p1), two_product(2.0 * p0, p2)), m3),
            (two_product(2.0 * p1, p2), m4),
            (two_product(p2, p2), m5),
        )
    )
    alpha2 = norm2 / curve2
    return alpha0 + alpha1 * grow + alpha2 * p0, alpha2 * p1 - alpha1 * alpha0, alpha2 * p2


def finish(sums, early_field, field, base, slopes, adjoint_hbm, gradient_hbm, adjoint, gradient, lam, sems):
    lane = tile_iota(1)
    copies = []
    scale = []
    for c in coefficients(sums):
        scale.append([jnp.sum(jnp.where(lane == 4 * i, c, 0.0), axis=1, keepdims=True) for i in range(3)])
    for i in range(3):
        for x in range(LAYERS + 2):
            for t in range(2):
                if t == 1 and x in (0, LAYERS + 1):
                    continue
                at = x + HALO - 1
                v = [(early_field if at in inner(k) else field)[k, i, at, t] for k in range(3)]
                value = scale[0][i] * v[0] + scale[1][i] * v[1] + scale[2][i] * v[2]
                lam[i, x, t] = value
                if t == 0 and 0 < x <= LAYERS:
                    adjoint[i, x - 1] = value
        copies.append(pltpu.make_async_copy(adjoint.at[i], adjoint_hbm.at[i], sems.at[i]))
        copies[-1].start()

    for x in range(1, LAYERS + 1):
        total = base[x - 1]
        for j in range(3):
            pair = (lam[j, x, 0], lam[j, x, 1])
            here = pair[0]
            around = (
                (lam[j, x + 1, 0], lam[j, x - 1, 0]),
                (z_next(pair)[0], z_prev(pair)[0]),
                (y_next(here), y_prev(here)),
            )
            for d, (after, before) in enumerate(around):
                total = total - (after - here) * slopes[d, 0, j, x - 1] - (here - before) * slopes[d, 1, j, x - 1]
        gradient[x - 1] = total
        if x % HALO == 0:
            part = pl.ds(x - HALO, HALO)
            copies.append(pltpu.make_async_copy(gradient.at[part], gradient_hbm.at[part], sems.at[2 + x // HALO]))
            copies[-1].start()
    for copy in copies:
        copy.wait()


def swap_a(axis):
    return [(i, i ^ 1) for i in range(lax.axis_size(axis))]


def swap_b(axis):
    count = lax.axis_size(axis)
    return [(i, (i + 1 if i % 2 else i - 1) % count) for i in range(count)]


def in_hbm(*arrays):
    return [pltpu.with_memory_space_constraint(a, pltpu.HBM) for a in arrays]


def shards(labels, table, factor, chi, weights):
    assert factor.shape == (LAYERS, 8, 128)
    assert lax.axis_size("col") % 2 == 0 and lax.axis_size("slab") % 2 == 0
    peers = lax.axis_size("col") * lax.axis_size("slab")
    f32 = functools.partial(jax.ShapeDtypeStruct, dtype=jnp.float32)
    scratch = functools.partial(pltpu.VMEM, dtype=jnp.float32)
    block = (4, LAYERS, 8, 128)
    half_block = f32((4, HALO, 8, 128))
    corner = f32((4, 2, 8, 128))
    fields = f32((3, 3, TOTAL, 2, 8, 128))

    own, x_a, x_b, z_a, z_b, splat = pl.pallas_call(
        prepare,
        out_shape=(f32(block),) + (half_block,) * 4 + (f32((9, 8, 128)),),
        in_specs=[HBM] * 5,
        out_specs=(VMEM,) * 6,
        scratch_shapes=[
            pltpu.VMEM((LAYERS, 8, 128), jnp.int32),
            pltpu.SMEM((3,), jnp.float32),
            scratch((LAYERS, 8, 128)),
            pltpu.SMEM((3, 3), jnp.float32),
            pltpu.SemaphoreType.DMA((7,)),
        ],
        compiler_params=PARAMS,
        name="prepare",
    )(*in_hbm(labels, table, factor, chi, weights))

    z_b = lax.ppermute(z_b, "slab", swap_b("slab"))
    z_a = lax.ppermute(z_a, "slab", swap_a("slab"))
    x_b = lax.ppermute(x_b, "col", swap_b("col"))
    x_a = lax.ppermute(x_a, "col", swap_a("col"))

    ring, corner_a, corner_b = pl.pallas_call(
        fold,
        out_shape=(f32(block), corner, corner),
        in_specs=[VMEM] * 2,
        out_specs=(VMEM,) * 3,
        compiler_params=PARAMS,
        name="fold",
    )(z_a, z_b)
    corner_b = lax.ppermute(corner_b, "col", swap_b("col"))
    corner_a = lax.ppermute(corner_a, "col", swap_a("col"))

    halo, cond, early_field, base, slopes = pl.pallas_call(
        early,
        out_shape=(
            f32(block),
            f32((3, TOTAL, 2, 8, 128)),
            fields,
            f32((LAYERS, 8, 128)),
            f32((3, 2, 3, LAYERS, 8, 128)),
        ),
        in_specs=[VMEM] * 5,
        out_specs=(VMEM,) * 5,
        compiler_params=PARAMS,
        name="early",
    )(own, ring, x_a, x_b, splat)

    field, sums = pl.pallas_call(
        functools.partial(krylov, peers),
        out_shape=(fields, f32((peers, 128))),
        in_specs=[VMEM] * 8,
        out_specs=(VMEM,) * 2,
        scratch_shapes=[scratch(block), scratch((3, TOTAL, 2, 8, 128))],
        compiler_params=PARAMS,
        name="krylov",
    )(own, ring, halo, corner_a, corner_b, splat, cond, early_field)

    gathered = lax.all_to_all(sums, ("col", "slab"), 0, 0, tiled=True)

    return pl.pallas_call(
        finish,
        out_shape=(f32((3, LAYERS, 8, 128)), f32((LAYERS, 8, 128))),
        in_specs=[VMEM] * 5,
        out_specs=(HBM,) * 2,
        scratch_shapes=[
            scratch((3, LAYERS, 8, 128)),
            scratch((LAYERS, 8, 128)),
            scratch((3, LAYERS + 2, 2, 8, 128)),
            pltpu.SemaphoreType.DMA((5,)),
        ],
        compiler_params=PARAMS,
        name="finish",
    )(gathered, early_field, field, base, slopes)


def solution(mesh):
    in_specs = (
        P("col", "slab", None),
        P(),
        P("col", "slab", None),
        P(None, "col", "slab", None),
        P(),
    )
    out_specs = (P(None, "col", "slab", None), P("col", "slab", None))
    return jax.shard_map(shards, mesh=mesh, in_specs=in_specs, out_specs=out_specs, check_vma=False)
```

```python
import functools

import jax
import jax.numpy as jnp
from jax import lax
from jax.experimental import pallas as pl
from jax.experimental.pallas import tpu as pltpu
from jax.sharding import PartitionSpec as P


mass_shift = 0.01
HALO = 4
MOMENTS = 6

VMEM = pl.BlockSpec(memory_space=pltpu.VMEM)
HBM = pl.BlockSpec(memory_space=pltpu.HBM)
PARAMS = pltpu.CompilerParams(vmem_limit_bytes=8 * 2**20)


def tile_iota(axis):
    return lax.broadcasted_iota(jnp.int32, (8, 128), axis)


def y_next(tile):
    return pltpu.roll(tile, 127, 1)


def y_prev(tile):
    return pltpu.roll(tile, 1, 1)


def z_next(pair):
    last = tile_iota(0) == 7
    first, second = (pltpu.roll(tile, 7, 0) for tile in pair)
    return jnp.where(last, second, first), jnp.where(last, first, second)


def z_prev(pair):
    top = tile_iota(0) == 0
    first, second = (pltpu.roll(tile, 1, 0) for tile in pair)
    return jnp.where(top, second, first), jnp.where(top, first, second)


def parity(axis):
    return lax.rem(lax.axis_index(axis), 2)


def choose(odd, if_even, if_odd):
    return jnp.where(jnp.full((8, 128), odd, jnp.int32) == 0, if_even, if_odd)


def prepare(
    labels_hbm, table_hbm, factor_hbm, chi_hbm, weights_hbm, own, x_a, x_b, z_a, z_b, splat,
    labels, table, factor, weights, sems,
):
    odd_col = parity("col")
    moves = [(table_hbm, table), (weights_hbm, weights)]
    for n in range(2):
        part = pl.ds(HALO * n, HALO)
        moves += [(chi_hbm.at[j, part], own.at[j, part]) for j in range(3)]
        moves += [(labels_hbm.at[part], labels.at[part]), (factor_hbm.at[part], factor.at[part])]
    copies = [pltpu.make_async_copy(source, target, sems.at[n]) for n, (source, target) in enumerate(moves)]
    for copy in copies:
        copy.start()
    for copy in copies:
        copy.wait()
    for x in range(2 * HALO):
        label = labels[x]
        own[3, x] = jnp.where(label == 0, table[0], jnp.where(label == 1, table[1], table[2])) * factor[x]
    for f in range(4):
        for x in range(HALO):
            low, high = own[f, x], own[f, HALO + x]
            x_a[f, x] = choose(odd_col, high, low)
            x_b[f, x] = choose(odd_col, low, high)
    for i in range(3):
        for j in range(3):
            splat[3 * i + j] = jnp.full((8, 128), weights[i, j], jnp.float32)
    odd_slab = parity("slab")
    half = tile_iota(0) < 4
    for f in range(4):
        for i in range(HALO):
            even, odd = own[f, 2 * i], own[f, 2 * i + 1]
            low_rows = jnp.where(half, even, pltpu.roll(odd, 4, 0))
            high_rows = jnp.where(half, pltpu.roll(even, 4, 0), odd)
            z_a[f, i] = choose(odd_slab, high_rows, low_rows)
            z_b[f, i] = choose(odd_slab, low_rows, high_rows)


def fold(z_b, z_a, ring, corner_a, corner_b):
    odd_col, odd_slab = parity("col"), parity("slab")
    half = tile_iota(0) < 4
    outer = (tile_iota(0) < 2) | (tile_iota(0) >= 6)

    def packed(first, second, third):
        return first, jnp.where(outer, second, jnp.where(half, pltpu.roll(third, 2, 0), pltpu.roll(third, 6, 0)))

    for f in range(4):
        tiles = []
        for i in range(HALO):
            up, down = choose(odd_slab, z_a[f, i], z_b[f, i]), choose(odd_slab, z_b[f, i], z_a[f, i])
            tiles.append(jnp.where(half, up, pltpu.roll(down, 4, 0)))
            tiles.append(jnp.where(half, pltpu.roll(up, 4, 0), down))
        for x, tile in enumerate(tiles):
            ring[f, x] = tile
        for n, (low, high) in enumerate(zip(packed(*tiles[:3]), packed(*tiles[:-4:-1]))):
            corner_a[f, n] = choose(odd_col, high, low)
            corner_b[f, n] = choose(odd_col, low, high)


def two_sum(a, b):
    total = a + b
    part = total - a
    return total, (a - (total - part)) + (b - part)


def two_product(a, b):
    product = a * b
    a_top, b_top = [4097.0 * v - (4097.0 * v - v) for v in (a, b)]
    a_rest, b_rest = a - a_top, b - b_top
    return product, ((a_top * b_top - product) + a_top * b_rest + a_rest * b_top) + a_rest * b_rest


def pair_sum(a, b):
    total, error = two_sum(a[0], b[0])
    return total, error + (a[1] + b[1])


def pair_product(a, b):
    product, error = two_product(a[0], b[0])
    return product, error + (a[0] * b[1] + a[1] * b[0])


def total_row(tiles):
    row = tile_iota(0)
    lane = tile_iota(1)
    pairs = [(tile, jnp.zeros((8, 128), jnp.float32)) for tile in tiles]
    place = [[n] for n in range(len(tiles))]
    for width in (4, 2, 1):
        lower = (row & width) == 0
        merged, spots = [], []
        for n in range(0, len(pairs), 2):
            first, second = pairs[n], pairs[min(n + 1, len(pairs) - 1)]
            kept = [jnp.where(lower, a, b) for a, b in zip(first, second)]
            moved = [jnp.where(lower, pltpu.roll(a, 8 - width, 0), pltpu.roll(b, width, 0)) for a, b in zip(first, second)]
            merged.append(pair_sum(kept, moved))
            spots.append((place[n], place[n + 1] if n + 1 < len(pairs) else None))
        pairs, place = merged, spots
    result = jnp.zeros((8, 128), jnp.float32)

    def home(spot, at, width):
        if spot is None:
            return
        if len(spot) == 1:
            yield spot[0], at
            return
        yield from home(spot[0], at, 2 * width)
        yield from home(spot[1], at + width, 2 * width)

    for pair, spot in zip(pairs, place):
        for shift in (64, 32, 16, 8, 4, 2, 1):
            pair = pair_sum(pair, [pltpu.roll(a, shift, 1) for a in pair])
        for n, at in home(spot, 0, 1):
            result = jnp.where((row == at) & (lane == 4 * n), pair[0], result)
            result = jnp.where((row == at) & (lane == 4 * n + 1), pair[1], result)
    return jnp.sum(result, axis=0, keepdims=True)


LAYERS = 2 * HALO
TOTAL = 2 * LAYERS


PAIRS = ((0, 0), (0, 1), (1, 1), (1, 2), (2, 2), (2, 3))


def needed(k, t):
    return range(1 + k + t, TOTAL - 1 - k - t)


def inner(k, t):
    return range(HALO + k + t, HALO + LAYERS - k - t)


def harmonic(here, after):
    return 2.0 * here * after / (here + after)


def keep_y(cond, x, t, here):
    value = harmonic(here, y_next(here))
    cond[2, x, t] = value
    cond[4, x, t] = y_prev(value)


def keep_z(cond, x, here):
    values = [harmonic(tile, beside) for tile, beside in zip(here, z_next(here))]
    for t, before in enumerate(z_prev(values)):
        cond[1, x, t] = values[t]
        cond[3, x, t] = before


def out_flow(x, tiles, value, cond, offset, fluxes):
    def x_flux(face, t):
        if (face, t) not in fluxes:
            fluxes[face, t] = cond(0, face, t) * (offset[0] + (value(face + 1, t) - value(face, t)))
        return fluxes[face, t]

    here = [value(x, t) for t in range(2)]
    above, below = z_next(here), z_prev(here)
    added = {}
    for t in tiles:
        z_part = cond(3, x, t) * (offset[1] + (here[t] - below[t])) - cond(1, x, t) * (offset[1] + (above[t] - here[t]))
        y_part = cond(4, x, t) * (offset[2] + (here[t] - y_prev(here[t]))) - cond(2, x, t) * (
            offset[2] + (y_next(here[t]) - here[t])
        )
        added[t] = (x_flux(x - 1, t) - x_flux(x, t)) + z_part + y_part
    return added


def both(read, *index):
    return [read(*index, t) for t in range(2)]


def by_layer(wanted):
    for x in range(TOTAL):
        tiles = [t for t in range(2) if wanted(x, t)]
        if tiles:
            yield x, tiles


def add_source(wanted, grid, cond, splat, field):
    offset = [[1.0 if d == j else 0.0 for d in range(3)] for j in range(3)]
    fluxes = [{} for _ in range(3)]
    for x, tiles in by_layer(wanted):
        drive = [
            out_flow(x, tiles, functools.partial(grid, j), cond, offset[j], fluxes[j]) for j in range(3)
        ]
        for i in range(3):
            for t in tiles:
                field[0, i, x, t] = (
                    splat[3 * i] * drive[0][t] + splat[3 * i + 1] * drive[1][t] + splat[3 * i + 2] * drive[2][t]
                )


def applied(k, i, wanted, v, cond):
    fluxes = {}
    value = functools.partial(v, k, i)
    for x, tiles in by_layer(wanted):
        added = out_flow(x, tiles, value, cond, (0.0, 0.0, 0.0), fluxes)
        yield x, {t: mass_shift * value(x, t) + added[t] for t in tiles}


def add_moments(partial, wanted, v, last):
    for i in range(3):
        for x in range(HALO, HALO + LAYERS):
            for m, (a, b) in enumerate(PAIRS):
                if wanted(b, x):
                    product = v(a, i, x, 0) * (last[i, x] if b == 3 else v(b, i, x, 0))
                    key = 3 * m + i
                    partial[key] = product if partial.get(key) is None else partial[key] + product


def face_parts(d, here, after, chi_here, chi_after, splat):
    local = [(1.0 if j == d else 0.0) + (chi_after[j] - chi_here[j]) for j in range(3)]
    energy = None
    for i in range(3):
        part = local[i] * (splat[3 * i] * local[0] + splat[3 * i + 1] * local[1] + splat[3 * i + 2] * local[2])
        energy = part if energy is None else energy + part
    inverse = 1.0 / (here + after)
    share = after * inverse
    rest = here * inverse
    now, back = 2.0 * share * share, 2.0 * rest * rest
    return [energy * now] + [value * now for value in local], [energy * back] + [value * back for value in local]


def early(own, ring, x_b, x_a, splat, halo, cond, field, base, slopes, moments):
    odd_col = parity("col")
    for f in range(4):
        for n in range(HALO):
            halo[f, n] = choose(odd_col, x_b[f, n], x_a[f, n])
            halo[f, HALO + n] = choose(odd_col, x_a[f, n], x_b[f, n])

    def grid(f, x, t):
        if t == 1:
            return ring[f, x - HALO]
        if x < HALO:
            return halo[f, x]
        return own[f, x - HALO] if x < HALO + LAYERS else halo[f, x - LAYERS]

    for x in range(TOTAL):
        here = grid(3, x, 0)
        keep_y(cond, x, 0, here)
        if x + 1 < TOTAL:
            cond[0, x, 0] = harmonic(here, grid(3, x + 1, 0))
        if HALO <= x < HALO + LAYERS:
            other = grid(3, x, 1)
            keep_y(cond, x, 1, other)
            if x + 1 < HALO + LAYERS:
                cond[0, x, 1] = harmonic(other, grid(3, x + 1, 1))
            keep_z(cond, x, (here, other))

    def ready(*index):
        return cond[index]

    def v(*index):
        return field[index]

    add_source(lambda x, t: x in inner(0, t), grid, ready, splat, field)
    for k in (1, 2):
        for i in range(3):
            for x, value in applied(k - 1, i, lambda x, t: x in inner(k, t), v, ready):
                for t in value:
                    field[k, i, x, t] = value[t]
    last = {}
    for i in range(3):
        for x, value in applied(2, i, lambda x, t: t == 0 and x in inner(3, 0), v, ready):
            last[i, x] = value[0]
    partial = {}
    add_moments(partial, lambda k, x: x in inner(k, 0), v, last)
    for n, value in partial.items():
        moments[n] = value

    carried = None
    for x in range(HALO - 1, HALO + LAYERS):
        here, after = [[grid(f, n, 0) for f in range(4)] for n in (x, x + 1)]
        now, back = face_parts(0, here[3], after[3], here[:3], after[:3], splat)
        if carried is not None:
            beside = [y_next(tile) for tile in here]
            y_now, y_back = face_parts(2, here[3], beside[3], here[:3], beside[:3], splat)
            y_back = [y_prev(tile) for tile in y_back]
            pairs = [(here[f], grid(f, x, 1)) for f in range(4)]
            nexts = [z_next(pair) for pair in pairs]
            z_now, z_back = zip(
                *[
                    face_parts(1, pairs[3][t], nexts[3][t], [p[t] for p in pairs[:3]], [p[t] for p in nexts[:3]], splat)
                    for t in range(2)
                ]
            )
            z_now, z_back = z_now[0], [z_prev(pair)[0] for pair in zip(*z_back)]
            sides = ((now, carried), (z_now, z_back), (y_now, y_back))
            base[x - HALO] = sum(side[0] for pair in sides for side in pair)
            for d in range(3):
                for n in range(2):
                    for j in range(3):
                        slopes[d, n, j, x - HALO] = sides[d][n][1 + j]
        carried = back


def krylov(
    peers, own, z_ring, halo, corner_b, corner_a, splat, early_cond, early_field, moments, field, sums, ring, cond
):
    odd_col = parity("col")
    half = tile_iota(0) < 4
    for f in range(4):
        tiles = [(corner_a[f, n], corner_b[f, n]) for n in range(2)]
        low = [choose(odd_col, b, a) for a, b in tiles]
        high = [choose(odd_col, a, b) for a, b in tiles]
        for (first, shared), spots in ((low, (3, 2, 1, 0)), (high, (4, 5, 6, 7))):
            third = jnp.where(half, pltpu.roll(shared, 6, 0), pltpu.roll(shared, 2, 0))
            for spot, tile in zip(spots, (first, shared, third, third)):
                ring[f, spot] = tile

    def grid(f, x, t):
        if x < HALO:
            return (halo, ring)[t][f, x]
        if x < HALO + LAYERS:
            return (own, z_ring)[t][f, x - HALO]
        return (halo, ring)[t][f, x - LAYERS]

    def is_early(d, x, t):
        return HALO <= x < HALO + LAYERS - (1 if d == 0 and t == 1 else 0) or (t == 0 and d in (0, 2, 4))

    def ready(d, x, t):
        return (early_cond if is_early(d, x, t) else cond)[d, x, t]

    def v(k, i, x, t):
        return (early_field if x in inner(k, t) else field)[k, i, x, t]

    for x in range(1, TOTAL - 1):
        if x < TOTAL - 2 and not is_early(0, x, 1):
            cond[0, x, 1] = harmonic(grid(3, x, 1), grid(3, x + 1, 1))
        if x in needed(0, 1) and not is_early(2, x, 1):
            keep_y(cond, x, 1, grid(3, x, 1))
        if not is_early(1, x, 1):
            keep_z(cond, x, both(grid, 3, x))

    add_source(lambda x, t: x in needed(0, t) and x not in inner(0, t), grid, ready, splat, field)
    for k in (1, 2):
        for i in range(3):
            for x, value in applied(k - 1, i, lambda x, t: x in needed(k, t) and x not in inner(k, t), v, ready):
                for t in value:
                    field[k, i, x, t] = value[t]
    last = {}
    for i in range(3):
        for x, value in applied(2, i, lambda x, t: t == 0 and x in needed(3, 0) and x not in inner(3, 0), v, ready):
            last[i, x] = value[0]
    partial = {n: moments[n] for n in range(3 * MOMENTS)}
    add_moments(partial, lambda k, x: x not in inner(k, 0), v, last)
    sums[...] = jnp.broadcast_to(total_row([partial[n] for n in range(3 * MOMENTS)]), (peers, 128))


def quadratic(terms):
    products = [pair_product(a, b) for a, b in terms]
    total = products[0]
    for product in products[1:]:
        total = pair_sum(total, product)
    return total[0] + total[1]


def coefficients(sums):
    count = sums.shape[0] // 8
    pairs = [(sums[8 * n : 8 * n + 8], jnp.zeros((8, 128), jnp.float32)) for n in range(count)]
    while len(pairs) > 1:
        tail = pairs[len(pairs) // 2 * 2 :]
        pairs = [pair_sum(pairs[n], pairs[n + 1]) for n in range(0, len(pairs) - 1, 2)] + tail
    pair = pairs[0]
    for shift in (4, 2, 1):
        pair = pair_sum(pair, [pltpu.roll(a, shift, 0) for a in pair])
    value, error = pair[0], pair[1] + pltpu.roll(pair[0], 127, 1)

    def moment(m):
        if m == 0:
            return value, error
        return pltpu.roll(value, 128 - 12 * m, 1), pltpu.roll(error, 128 - 12 * m, 1)

    m0, m1, m2, m3, m4, m5 = [moment(m) for m in range(MOMENTS)]
    none = jnp.zeros((8, 128), jnp.float32)
    one = (jnp.ones((8, 128), jnp.float32), none)
    alpha0 = m0[0] / m1[0]
    inverse0 = 1.0 / m0[0]
    alpha0_squared = two_product(alpha0, alpha0)
    norm1 = quadratic(((one, m0), ((-2.0 * alpha0, none), m1), (alpha0_squared, m2)))
    inverse1 = 1.0 / norm1
    grow = 1.0 + norm1 * inverse0
    curve1 = quadratic(
        ((two_product(grow, grow), m1), (two_product(-2.0 * grow, alpha0), m2), (alpha0_squared, m3))
    )
    alpha1 = norm1 / curve1
    r1 = -(alpha0 + alpha1 * grow)
    r2 = alpha1 * alpha0
    norm2 = quadratic(
        (
            (one, m0),
            ((2.0 * r1, none), m1),
            (pair_sum(two_product(r1, r1), (2.0 * r2, none)), m2),
            (two_product(2.0 * r1, r2), m3),
            (two_product(r2, r2), m4),
        )
    )
    beta1 = norm2 * inverse1
    p0, p1, p2 = 1.0 + beta1 * grow, r1 - beta1 * alpha0, r2
    curve2 = quadratic(
        (
            (two_product(p0, p0), m1),
            (two_product(2.0 * p0, p1), m2),
            (pair_sum(two_product(p1, p1), two_product(2.0 * p0, p2)), m3),
            (two_product(2.0 * p1, p2), m4),
            (two_product(p2, p2), m5),
        )
    )
    alpha2 = norm2 / curve2
    return alpha0 + alpha1 * grow + alpha2 * p0, alpha2 * p1 - alpha1 * alpha0, alpha2 * p2


def finish(sums, early_field, field, base, slopes, adjoint_hbm, gradient_hbm, adjoint, gradient, lam, sems):
    lane = tile_iota(1)
    copies = []
    scale = []
    for c in coefficients(sums):
        scale.append([jnp.sum(jnp.where(lane == 4 * i, c, 0.0), axis=1, keepdims=True) for i in range(3)])
    for i in range(3):
        for x in range(LAYERS + 2):
            for t in range(2):
                if t == 1 and x in (0, LAYERS + 1):
                    continue
                at = x + HALO - 1
                v = [(early_field if at in inner(k, t) else field)[k, i, at, t] for k in range(3)]
                value = scale[0][i] * v[0] + scale[1][i] * v[1] + scale[2][i] * v[2]
                lam[i, x, t] = value
                if t == 0 and 0 < x <= LAYERS:
                    adjoint[i, x - 1] = value
        copies.append(pltpu.make_async_copy(adjoint.at[i], adjoint_hbm.at[i], sems.at[i]))
        copies[-1].start()

    for x in range(1, LAYERS + 1):
        total = base[x - 1]
        for j in range(3):
            pair = (lam[j, x, 0], lam[j, x, 1])
            here = pair[0]
            around = (
                (lam[j, x + 1, 0], lam[j, x - 1, 0]),
                (z_next(pair)[0], z_prev(pair)[0]),
                (y_next(here), y_prev(here)),
            )
            for d, (after, before) in enumerate(around):
                total = total - (after - here) * slopes[d, 0, j, x - 1] - (here - before) * slopes[d, 1, j, x - 1]
        gradient[x - 1] = total
        if x % HALO == 0:
            part = pl.ds(x - HALO, HALO)
            copies.append(pltpu.make_async_copy(gradient.at[part], gradient_hbm.at[part], sems.at[2 + x // HALO]))
            copies[-1].start()
    for copy in copies:
        copy.wait()


def swap_a(axis):
    return [(i, i ^ 1) for i in range(lax.axis_size(axis))]


def swap_b(axis):
    count = lax.axis_size(axis)
    return [(i, (i + 1 if i % 2 else i - 1) % count) for i in range(count)]


def in_hbm(*arrays):
    return [pltpu.with_memory_space_constraint(a, pltpu.HBM) for a in arrays]


def shards(labels, table, factor, chi, weights):
    assert factor.shape == (LAYERS, 8, 128)
    assert lax.axis_size("col") % 2 == 0 and lax.axis_size("slab") % 2 == 0
    peers = lax.axis_size("col") * lax.axis_size("slab")
    f32 = functools.partial(jax.ShapeDtypeStruct, dtype=jnp.float32)
    scratch = functools.partial(pltpu.VMEM, dtype=jnp.float32)
    block = (4, LAYERS, 8, 128)
    half_block = f32((4, HALO, 8, 128))
    corner = f32((4, 2, 8, 128))
    fields = f32((3, 3, TOTAL, 2, 8, 128))

    own, x_a, x_b, z_a, z_b, splat = pl.pallas_call(
        prepare,
        out_shape=(f32(block),) + (half_block,) * 4 + (f32((9, 8, 128)),),
        in_specs=[HBM] * 5,
        out_specs=(VMEM,) * 6,
        scratch_shapes=[
            pltpu.VMEM((LAYERS, 8, 128), jnp.int32),
            pltpu.SMEM((3,), jnp.float32),
            scratch((LAYERS, 8, 128)),
            pltpu.SMEM((3, 3), jnp.float32),
            pltpu.SemaphoreType.DMA((12,)),
        ],
        compiler_params=PARAMS,
        name="prepare",
    )(*in_hbm(labels, table, factor, chi, weights))

    z_b = lax.ppermute(z_b, "slab", swap_b("slab"))
    z_a = lax.ppermute(z_a, "slab", swap_a("slab"))
    x_b = lax.ppermute(x_b, "col", swap_b("col"))
    x_a = lax.ppermute(x_a, "col", swap_a("col"))

    ring, corner_a, corner_b = pl.pallas_call(
        fold,
        out_shape=(f32(block), corner, corner),
        in_specs=[VMEM] * 2,
        out_specs=(VMEM,) * 3,
        compiler_params=PARAMS,
        name="fold",
    )(z_b, z_a)
    corner_b = lax.ppermute(corner_b, "col", swap_b("col"))
    corner_a = lax.ppermute(corner_a, "col", swap_a("col"))

    halo, cond, early_field, base, slopes, moments = pl.pallas_call(
        early,
        out_shape=(
            f32(block),
            f32((5, TOTAL, 2, 8, 128)),
            fields,
            f32((LAYERS, 8, 128)),
            f32((3, 2, 3, LAYERS, 8, 128)),
            f32((3 * MOMENTS, 8, 128)),
        ),
        in_specs=[VMEM] * 5,
        out_specs=(VMEM,) * 6,
        compiler_params=PARAMS,
        name="early",
    )(own, ring, x_b, x_a, splat)

    field, sums = pl.pallas_call(
        functools.partial(krylov, peers),
        out_shape=(fields, f32((peers, 128))),
        in_specs=[VMEM] * 9,
        out_specs=(VMEM,) * 2,
        scratch_shapes=[scratch(block), scratch((5, TOTAL, 2, 8, 128))],
        compiler_params=PARAMS,
        name="krylov",
    )(own, ring, halo, corner_b, corner_a, splat, cond, early_field, moments)

    gathered = lax.all_to_all(sums, ("col", "slab"), 0, 0, tiled=True)

    return pl.pallas_call(
        finish,
        out_shape=(f32((3, LAYERS, 8, 128)), f32((LAYERS, 8, 128))),
        in_specs=[VMEM] * 5,
        out_specs=(HBM,) * 2,
        scratch_shapes=[
            scratch((3, LAYERS, 8, 128)),
            scratch((LAYERS, 8, 128)),
            scratch((3, LAYERS + 2, 2, 8, 128)),
            pltpu.SemaphoreType.DMA((5,)),
        ],
        compiler_params=PARAMS,
        name="finish",
    )(gathered, early_field, field, base, slopes)


def solution(mesh):
    in_specs = (
        P("col", "slab", None),
        P(),
        P("col", "slab", None),
        P(None, "col", "slab", None),
        P(),
    )
    out_specs = (P(None, "col", "slab", None), P("col", "slab", None))
    return jax.shard_map(shards, mesh=mesh, in_specs=in_specs, out_specs=out_specs, check_vma=False)
```

```python
import functools

import jax
import jax.numpy as jnp
from jax import lax
from jax.experimental import pallas as pl
from jax.experimental.pallas import tpu as pltpu
from jax.sharding import PartitionSpec as P


mass_shift = 0.01
HALO = 4
MOMENTS = 6
NORM_FLOOR = 1e-14

VMEM = pl.BlockSpec(memory_space=pltpu.VMEM)
HBM = pl.BlockSpec(memory_space=pltpu.HBM)
PARAMS = pltpu.CompilerParams(vmem_limit_bytes=8 * 2**20)


def tile_iota(axis):
    return lax.broadcasted_iota(jnp.int32, (8, 128), axis)


def y_next(tile):
    return pltpu.roll(tile, 127, 1)


def y_prev(tile):
    return pltpu.roll(tile, 1, 1)


def z_next(pair):
    last = tile_iota(0) == 7
    first, second = (pltpu.roll(tile, 7, 0) for tile in pair)
    return jnp.where(last, second, first), jnp.where(last, first, second)


def z_prev(pair):
    top = tile_iota(0) == 0
    first, second = (pltpu.roll(tile, 1, 0) for tile in pair)
    return jnp.where(top, second, first), jnp.where(top, first, second)


def parity(axis):
    return lax.rem(lax.axis_index(axis), 2)


def choose(odd, if_even, if_odd):
    return jnp.where(jnp.full((8, 128), odd, jnp.int32) == 0, if_even, if_odd)


def prepare(
    labels_hbm, table_hbm, factor_hbm, chi_hbm, weights_hbm, own, x_a, x_b, z_a, z_b, splat,
    labels, table, factor, weights, sems,
):
    odd_col = parity("col")
    moves = [(chi_hbm.at[j], own.at[j]) for j in range(3)] + [(factor_hbm, factor), (labels_hbm, labels)]
    moves += [(table_hbm, table), (weights_hbm, weights)]
    copies = [pltpu.make_async_copy(source, target, sems.at[n]) for n, (source, target) in enumerate(moves)]
    for copy in copies:
        copy.start()
    for copy in copies:
        copy.wait()
    for x in range(2 * HALO):
        label = labels[x]
        own[3, x] = jnp.where(label == 0, table[0], jnp.where(label == 1, table[1], table[2])) * factor[x]
    for f in range(4):
        for x in range(HALO):
            low, high = own[f, x], own[f, HALO + x]
            x_a[f, x] = choose(odd_col, high, low)
            x_b[f, x] = choose(odd_col, low, high)
    for i in range(3):
        for j in range(3):
            splat[3 * i + j] = jnp.full((8, 128), weights[i, j], jnp.float32)
    odd_slab = parity("slab")
    half = tile_iota(0) < 4
    for f in range(4):
        for i in range(HALO):
            even, odd = own[f, 2 * i], own[f, 2 * i + 1]
            low_rows = jnp.where(half, even, pltpu.roll(odd, 4, 0))
            high_rows = jnp.where(half, pltpu.roll(even, 4, 0), odd)
            z_a[f, i] = choose(odd_slab, high_rows, low_rows)
            z_b[f, i] = choose(odd_slab, low_rows, high_rows)


def fold(z_b, z_a, ring, corner_a, corner_b):
    odd_col, odd_slab = parity("col"), parity("slab")
    half = tile_iota(0) < 4
    outer = (tile_iota(0) < 2) | (tile_iota(0) >= 6)

    def packed(first, second, third):
        return first, jnp.where(outer, second, jnp.where(half, pltpu.roll(third, 2, 0), pltpu.roll(third, 6, 0)))

    for f in range(4):
        tiles = []
        for i in range(HALO):
            up, down = choose(odd_slab, z_a[f, i], z_b[f, i]), choose(odd_slab, z_b[f, i], z_a[f, i])
            tiles.append(jnp.where(half, up, pltpu.roll(down, 4, 0)))
            tiles.append(jnp.where(half, pltpu.roll(up, 4, 0), down))
        for x, tile in enumerate(tiles):
            ring[f, x] = tile
        for n, (low, high) in enumerate(zip(packed(*tiles[:3]), packed(*tiles[:-4:-1]))):
            corner_a[f, n] = choose(odd_col, high, low)
            corner_b[f, n] = choose(odd_col, low, high)


def two_sum(a, b):
    total = a + b
    part = total - a
    return total, (a - (total - part)) + (b - part)


def split(value):
    scaled = 4097.0 * value
    top = scaled - (scaled - value)
    return top, value - top


def exact_product(a, a_parts, b, b_parts):
    product = a * b
    (a_top, a_rest), (b_top, b_rest) = a_parts, b_parts
    return product, ((a_top * b_top - product) + a_top * b_rest + a_rest * b_top) + a_rest * b_rest


def two_product(a, b):
    return exact_product(a, split(a), b, split(b))


def pair_sum(a, b):
    total, error = two_sum(a[0], b[0])
    return total, error + (a[1] + b[1])


def pair_product(a, b):
    product, error = two_product(a[0], b[0])
    return product, error + (a[0] * b[1] + a[1] * b[0])


def total_row(pairs):
    row = tile_iota(0)
    lane = tile_iota(1)
    place = [[n] for n in range(len(pairs))]
    for width in (4, 2, 1):
        lower = (row & width) == 0
        merged, spots = [], []
        for n in range(0, len(pairs), 2):
            first, second = pairs[n], pairs[min(n + 1, len(pairs) - 1)]
            kept = [jnp.where(lower, a, b) for a, b in zip(first, second)]
            moved = [jnp.where(lower, pltpu.roll(a, 8 - width, 0), pltpu.roll(b, width, 0)) for a, b in zip(first, second)]
            merged.append(pair_sum(kept, moved))
            spots.append((place[n], place[n + 1] if n + 1 < len(pairs) else None))
        pairs, place = merged, spots
    result = jnp.zeros((8, 128), jnp.float32)

    def home(spot, at, width):
        if spot is None:
            return
        if len(spot) == 1:
            yield spot[0], at
            return
        yield from home(spot[0], at, 2 * width)
        yield from home(spot[1], at + width, 2 * width)

    for pair, spot in zip(pairs, place):
        for shift in (64, 32, 16, 8, 4, 2, 1):
            pair = pair_sum(pair, [pltpu.roll(a, shift, 1) for a in pair])
        for n, at in home(spot, 0, 1):
            result = jnp.where((row == at) & (lane == 4 * n), pair[0], result)
            result = jnp.where((row == at) & (lane == 4 * n + 1), pair[1], result)
    return jnp.sum(result, axis=0, keepdims=True)


LAYERS = 2 * HALO
TOTAL = 2 * LAYERS


PAIRS = ((0, 0), (0, 1), (1, 1), (1, 2), (2, 2), (2, 3))


def needed(k, t):
    return range(1 + k + t, TOTAL - 1 - k - t)


def inner(k, t):
    return range(HALO + k + t, HALO + LAYERS - k - t)


def harmonic(here, after):
    return 2.0 * here * after / (here + after)


def keep_y(cond, x, t, here):
    value = harmonic(here, y_next(here))
    cond[2, x, t] = value
    cond[4, x, t] = y_prev(value)


def keep_z(cond, x, here):
    values = [harmonic(tile, beside) for tile, beside in zip(here, z_next(here))]
    for t, before in enumerate(z_prev(values)):
        cond[1, x, t] = values[t]
        cond[3, x, t] = before


def out_flow(x, tiles, value, cond, offset, fluxes):
    def x_flux(face, t):
        if (face, t) not in fluxes:
            fluxes[face, t] = cond(0, face, t) * (offset[0] + (value(face + 1, t) - value(face, t)))
        return fluxes[face, t]

    here = [value(x, t) for t in range(2)]
    above, below = z_next(here), z_prev(here)
    added = {}
    for t in tiles:
        z_part = cond(3, x, t) * (offset[1] + (here[t] - below[t])) - cond(1, x, t) * (offset[1] + (above[t] - here[t]))
        y_part = cond(4, x, t) * (offset[2] + (here[t] - y_prev(here[t]))) - cond(2, x, t) * (
            offset[2] + (y_next(here[t]) - here[t])
        )
        added[t] = (x_flux(x - 1, t) - x_flux(x, t)) + z_part + y_part
    return added


def both(read, *index):
    return [read(*index, t) for t in range(2)]


def by_layer(wanted):
    for x in range(TOTAL):
        tiles = [t for t in range(2) if wanted(x, t)]
        if tiles:
            yield x, tiles


def add_source(wanted, grid, cond, splat, field):
    offset = [[1.0 if d == j else 0.0 for d in range(3)] for j in range(3)]
    fluxes = [{} for _ in range(3)]
    for x, tiles in by_layer(wanted):
        drive = [
            out_flow(x, tiles, functools.partial(grid, j), cond, offset[j], fluxes[j]) for j in range(3)
        ]
        for i in range(3):
            for t in tiles:
                field[0, i, x, t] = (
                    splat[3 * i] * drive[0][t] + splat[3 * i + 1] * drive[1][t] + splat[3 * i + 2] * drive[2][t]
                )


def applied(k, i, wanted, v, cond):
    fluxes = {}
    value = functools.partial(v, k, i)
    for x, tiles in by_layer(wanted):
        added = out_flow(x, tiles, value, cond, (0.0, 0.0, 0.0), fluxes)
        yield x, {t: mass_shift * value(x, t) + added[t] for t in tiles}


def add_moments(partial, wanted, v, last):
    for i in range(3):
        for x in range(HALO, HALO + LAYERS):
            pairs = [(m, pair) for m, pair in enumerate(PAIRS) if wanted(pair[1], x)]
            used = sorted({k for m, pair in pairs for k in pair})
            tiles = {k: last[i, x] if k == 3 else v(k, i, x, 0) for k in used}
            parts = {k: split(tiles[k]) for k in used}
            for m, (a, b) in pairs:
                product = exact_product(tiles[a], parts[a], tiles[b], parts[b])
                key = 3 * m + i
                partial[key] = pair_sum(partial[key], product) if key in partial else product


def face_parts(d, here, after, chi_here, chi_after, splat):
    local = [(1.0 if j == d else 0.0) + (chi_after[j] - chi_here[j]) for j in range(3)]
    energy = None
    for i in range(3):
        part = local[i] * (splat[3 * i] * local[0] + splat[3 * i + 1] * local[1] + splat[3 * i + 2] * local[2])
        energy = part if energy is None else energy + part
    inverse = 1.0 / (here + after)
    share = after * inverse
    rest = here * inverse
    now, back = 2.0 * share * share, 2.0 * rest * rest
    return [energy * now] + [value * now for value in local], [energy * back] + [value * back for value in local]


def early(own, ring, x_b, x_a, splat, halo, cond, field, base, slopes, moments):
    odd_col = parity("col")
    for f in range(4):
        for n in range(HALO):
            halo[f, n] = choose(odd_col, x_b[f, n], x_a[f, n])
            halo[f, HALO + n] = choose(odd_col, x_a[f, n], x_b[f, n])

    def grid(f, x, t):
        if t == 1:
            return ring[f, x - HALO]
        if x < HALO:
            return halo[f, x]
        return own[f, x - HALO] if x < HALO + LAYERS else halo[f, x - LAYERS]

    for x in range(TOTAL):
        here = grid(3, x, 0)
        keep_y(cond, x, 0, here)
        if x + 1 < TOTAL:
            cond[0, x, 0] = harmonic(here, grid(3, x + 1, 0))
        if HALO <= x < HALO + LAYERS:
            other = grid(3, x, 1)
            keep_y(cond, x, 1, other)
            if x + 1 < HALO + LAYERS:
                cond[0, x, 1] = harmonic(other, grid(3, x + 1, 1))
            keep_z(cond, x, (here, other))

    def ready(*index):
        return cond[index]

    def v(*index):
        return field[index]

    add_source(lambda x, t: x in inner(0, t), grid, ready, splat, field)
    for k in (1, 2):
        for i in range(3):
            for x, value in applied(k - 1, i, lambda x, t: x in inner(k, t), v, ready):
                for t in value:
                    field[k, i, x, t] = value[t]
    last = {}
    for i in range(3):
        for x, value in applied(2, i, lambda x, t: t == 0 and x in inner(3, 0), v, ready):
            last[i, x] = value[0]
    partial = {}
    add_moments(partial, lambda k, x: x in inner(k, 0), v, last)
    for n, pair in partial.items():
        moments[0, n], moments[1, n] = pair

    carried = None
    for x in range(HALO - 1, HALO + LAYERS):
        here, after = [[grid(f, n, 0) for f in range(4)] for n in (x, x + 1)]
        now, back = face_parts(0, here[3], after[3], here[:3], after[:3], splat)
        if carried is not None:
            beside = [y_next(tile) for tile in here]
            y_now, y_back = face_parts(2, here[3], beside[3], here[:3], beside[:3], splat)
            y_back = [y_prev(tile) for tile in y_back]
            pairs = [(here[f], grid(f, x, 1)) for f in range(4)]
            nexts = [z_next(pair) for pair in pairs]
            z_now, z_back = zip(
                *[
                    face_parts(1, pairs[3][t], nexts[3][t], [p[t] for p in pairs[:3]], [p[t] for p in nexts[:3]], splat)
                    for t in range(2)
                ]
            )
            z_now, z_back = z_now[0], [z_prev(pair)[0] for pair in zip(*z_back)]
            sides = ((now, carried), (z_now, z_back), (y_now, y_back))
            base[x - HALO] = sum(side[0] for pair in sides for side in pair)
            for d in range(3):
                for n in range(2):
                    for j in range(3):
                        slopes[d, n, j, x - HALO] = sides[d][n][1 + j]
        carried = back


def krylov(
    peers, own, z_ring, halo, corner_b, corner_a, splat, early_cond, early_field, moments, field, sums, ring, cond
):
    odd_col = parity("col")
    half = tile_iota(0) < 4
    for f in range(4):
        tiles = [(corner_a[f, n], corner_b[f, n]) for n in range(2)]
        low = [choose(odd_col, b, a) for a, b in tiles]
        high = [choose(odd_col, a, b) for a, b in tiles]
        for (first, shared), spots in ((low, (3, 2, 1, 0)), (high, (4, 5, 6, 7))):
            third = jnp.where(half, pltpu.roll(shared, 6, 0), pltpu.roll(shared, 2, 0))
            for spot, tile in zip(spots, (first, shared, third, third)):
                ring[f, spot] = tile

    def grid(f, x, t):
        if x < HALO:
            return (halo, ring)[t][f, x]
        if x < HALO + LAYERS:
            return (own, z_ring)[t][f, x - HALO]
        return (halo, ring)[t][f, x - LAYERS]

    def is_early(d, x, t):
        return HALO <= x < HALO + LAYERS - (1 if d == 0 and t == 1 else 0) or (t == 0 and d in (0, 2, 4))

    def ready(d, x, t):
        return (early_cond if is_early(d, x, t) else cond)[d, x, t]

    def v(k, i, x, t):
        return (early_field if x in inner(k, t) else field)[k, i, x, t]

    for x in range(1, TOTAL - 1):
        if x < TOTAL - 2 and not is_early(0, x, 1):
            cond[0, x, 1] = harmonic(grid(3, x, 1), grid(3, x + 1, 1))
        if x in needed(0, 1) and not is_early(2, x, 1):
            keep_y(cond, x, 1, grid(3, x, 1))
        if not is_early(1, x, 1):
            keep_z(cond, x, both(grid, 3, x))

    add_source(lambda x, t: x in needed(0, t) and x not in inner(0, t), grid, ready, splat, field)
    for k in (1, 2):
        for i in range(3):
            for x, value in applied(k - 1, i, lambda x, t: x in needed(k, t) and x not in inner(k, t), v, ready):
                for t in value:
                    field[k, i, x, t] = value[t]
    last = {}
    for i in range(3):
        for x, value in applied(2, i, lambda x, t: t == 0 and x in needed(3, 0) and x not in inner(3, 0), v, ready):
            last[i, x] = value[0]
    partial = {n: (moments[0, n], moments[1, n]) for n in range(3 * MOMENTS)}
    add_moments(partial, lambda k, x: x not in inner(k, 0), v, last)
    sums[...] = jnp.broadcast_to(total_row([partial[n] for n in range(3 * MOMENTS)]), (peers, 128))


def quadratic(terms):
    products = [pair_product(a, b) for a, b in terms]
    total = products[0]
    for product in products[1:]:
        total = pair_sum(total, product)
    return total[0] + total[1]


def coefficients(sums):
    count = sums.shape[0] // 8
    pairs = [(sums[8 * n : 8 * n + 8], jnp.zeros((8, 128), jnp.float32)) for n in range(count)]
    while len(pairs) > 1:
        tail = pairs[len(pairs) // 2 * 2 :]
        pairs = [pair_sum(pairs[n], pairs[n + 1]) for n in range(0, len(pairs) - 1, 2)] + tail
    pair = pairs[0]
    for shift in (4, 2, 1):
        pair = pair_sum(pair, [pltpu.roll(a, shift, 0) for a in pair])
    value, error = pair[0], pair[1] + pltpu.roll(pair[0], 127, 1)

    def moment(m):
        if m == 0:
            return value, error
        return pltpu.roll(value, 128 - 12 * m, 1), pltpu.roll(error, 128 - 12 * m, 1)

    m0, m1, m2, m3, m4, m5 = [moment(m) for m in range(MOMENTS)]
    none = jnp.zeros((8, 128), jnp.float32)
    one = (jnp.ones((8, 128), jnp.float32), none)
    alpha0 = m0[0] / m1[0]
    inverse0 = 1.0 / m0[0]
    alpha0_squared = two_product(alpha0, alpha0)
    norm1 = quadratic(((one, m0), ((-2.0 * alpha0, none), m1), (alpha0_squared, m2)))
    norm1 = jnp.maximum(norm1, NORM_FLOOR * m0[0])
    inverse1 = 1.0 / norm1
    grow = 1.0 + norm1 * inverse0
    curve1 = quadratic(
        ((two_product(grow, grow), m1), (two_product(-2.0 * grow, alpha0), m2), (alpha0_squared, m3))
    )
    alpha1 = norm1 / jnp.maximum(curve1, mass_shift * norm1)
    r1 = -(alpha0 + alpha1 * grow)
    r2 = alpha1 * alpha0
    norm2 = quadratic(
        (
            (one, m0),
            ((2.0 * r1, none), m1),
            (pair_sum(two_product(r1, r1), (2.0 * r2, none)), m2),
            (two_product(2.0 * r1, r2), m3),
            (two_product(r2, r2), m4),
        )
    )
    norm2 = jnp.maximum(norm2, NORM_FLOOR * norm1)
    beta1 = norm2 * inverse1
    p0, p1, p2 = 1.0 + beta1 * grow, r1 - beta1 * alpha0, r2
    curve2 = quadratic(
        (
            (two_product(p0, p0), m1),
            (two_product(2.0 * p0, p1), m2),
            (pair_sum(two_product(p1, p1), two_product(2.0 * p0, p2)), m3),
            (two_product(2.0 * p1, p2), m4),
            (two_product(p2, p2), m5),
        )
    )
    alpha2 = norm2 / jnp.maximum(curve2, mass_shift * norm2)
    return alpha0 + alpha1 * grow + alpha2 * p0, alpha2 * p1 - alpha1 * alpha0, alpha2 * p2


def finish(sums, early_field, field, base, slopes, adjoint_hbm, gradient_hbm, adjoint, gradient, lam, sems):
    lane = tile_iota(1)
    copies = []
    scale = []
    for c in coefficients(sums):
        scale.append([jnp.sum(jnp.where(lane == 4 * i, c, 0.0), axis=1, keepdims=True) for i in range(3)])
    for i in range(3):
        for x in range(LAYERS + 2):
            for t in range(2):
                if t == 1 and x in (0, LAYERS + 1):
                    continue
                at = x + HALO - 1
                v = [(early_field if at in inner(k, t) else field)[k, i, at, t] for k in range(3)]
                value = scale[0][i] * v[0] + scale[1][i] * v[1] + scale[2][i] * v[2]
                lam[i, x, t] = value
                if t == 0 and 0 < x <= LAYERS:
                    adjoint[i, x - 1] = value
        copies.append(pltpu.make_async_copy(adjoint.at[i], adjoint_hbm.at[i], sems.at[i]))
        copies[-1].start()

    for x in range(1, LAYERS + 1):
        total = base[x - 1]
        for j in range(3):
            pair = (lam[j, x, 0], lam[j, x, 1])
            here = pair[0]
            around = (
                (lam[j, x + 1, 0], lam[j, x - 1, 0]),
                (z_next(pair)[0], z_prev(pair)[0]),
                (y_next(here), y_prev(here)),
            )
            for d, (after, before) in enumerate(around):
                total = total - (after - here) * slopes[d, 0, j, x - 1] - (here - before) * slopes[d, 1, j, x - 1]
        gradient[x - 1] = total
        if x % HALO == 0:
            part = pl.ds(x - HALO, HALO)
            copies.append(pltpu.make_async_copy(gradient.at[part], gradient_hbm.at[part], sems.at[2 + x // HALO]))
            copies[-1].start()
    for copy in copies:
        copy.wait()


def swap_a(axis):
    return [(i, i ^ 1) for i in range(lax.axis_size(axis))]


def swap_b(axis):
    count = lax.axis_size(axis)
    return [(i, (i + 1 if i % 2 else i - 1) % count) for i in range(count)]


def in_hbm(*arrays):
    return [pltpu.with_memory_space_constraint(a, pltpu.HBM) for a in arrays]


def shards(labels, table, factor, chi, weights):
    assert factor.shape == (LAYERS, 8, 128)
    assert lax.axis_size("col") % 2 == 0 and lax.axis_size("slab") % 2 == 0
    peers = lax.axis_size("col") * lax.axis_size("slab")
    f32 = functools.partial(jax.ShapeDtypeStruct, dtype=jnp.float32)
    scratch = functools.partial(pltpu.VMEM, dtype=jnp.float32)
    block = (4, LAYERS, 8, 128)
    half_block = f32((4, HALO, 8, 128))
    corner = f32((4, 2, 8, 128))
    fields = f32((3, 3, TOTAL, 2, 8, 128))

    own, x_a, x_b, z_a, z_b, splat = pl.pallas_call(
        prepare,
        out_shape=(f32(block),) + (half_block,) * 4 + (f32((9, 8, 128)),),
        in_specs=[HBM] * 5,
        out_specs=(VMEM,) * 6,
        scratch_shapes=[
            pltpu.VMEM((LAYERS, 8, 128), jnp.int32),
            pltpu.SMEM((3,), jnp.float32),
            scratch((LAYERS, 8, 128)),
            pltpu.SMEM((3, 3), jnp.float32),
            pltpu.SemaphoreType.DMA((12,)),
        ],
        compiler_params=PARAMS,
        name="prepare",
    )(*in_hbm(labels, table, factor, chi, weights))

    z_b = lax.ppermute(z_b, "slab", swap_b("slab"))
    z_a = lax.ppermute(z_a, "slab", swap_a("slab"))
    x_b = lax.ppermute(x_b, "col", swap_b("col"))
    x_a = lax.ppermute(x_a, "col", swap_a("col"))

    ring, corner_a, corner_b = pl.pallas_call(
        fold,
        out_shape=(f32(block), corner, corner),
        in_specs=[VMEM] * 2,
        out_specs=(VMEM,) * 3,
        compiler_params=PARAMS,
        name="fold",
    )(z_b, z_a)
    corner_b = lax.ppermute(corner_b, "col", swap_b("col"))
    corner_a = lax.ppermute(corner_a, "col", swap_a("col"))

    halo, cond, early_field, base, slopes, moments = pl.pallas_call(
        early,
        out_shape=(
            f32(block),
            f32((5, TOTAL, 2, 8, 128)),
            fields,
            f32((LAYERS, 8, 128)),
            f32((3, 2, 3, LAYERS, 8, 128)),
            f32((2, 3 * MOMENTS, 8, 128)),
        ),
        in_specs=[VMEM] * 5,
        out_specs=(VMEM,) * 6,
        compiler_params=PARAMS,
        name="early",
    )(own, ring, x_b, x_a, splat)

    field, sums = pl.pallas_call(
        functools.partial(krylov, peers),
        out_shape=(fields, f32((peers, 128))),
        in_specs=[VMEM] * 9,
        out_specs=(VMEM,) * 2,
        scratch_shapes=[scratch(block), scratch((5, TOTAL, 2, 8, 128))],
        compiler_params=PARAMS,
        name="krylov",
    )(own, ring, halo, corner_b, corner_a, splat, cond, early_field, moments)

    gathered = lax.all_to_all(sums, ("col", "slab"), 0, 0, tiled=True)

    return pl.pallas_call(
        finish,
        out_shape=(f32((3, LAYERS, 8, 128)), f32((LAYERS, 8, 128))),
        in_specs=[VMEM] * 5,
        out_specs=(HBM,) * 2,
        scratch_shapes=[
            scratch((3, LAYERS, 8, 128)),
            scratch((LAYERS, 8, 128)),
            scratch((3, LAYERS + 2, 2, 8, 128)),
            pltpu.SemaphoreType.DMA((5,)),
        ],
        compiler_params=PARAMS,
        name="finish",
    )(gathered, early_field, field, base, slopes)


def solution(mesh):
    in_specs = (
        P("col", "slab", None),
        P(),
        P("col", "slab", None),
        P(None, "col", "slab", None),
        P(),
    )
    out_specs = (P(None, "col", "slab", None), P("col", "slab", None))
    return jax.shard_map(shards, mesh=mesh, in_specs=in_specs, out_specs=out_specs, check_vma=False)
```

```python
import functools

import jax
import jax.numpy as jnp
from jax import lax
from jax.experimental import pallas as pl
from jax.experimental.pallas import tpu as pltpu
from jax.sharding import PartitionSpec as P


mass_shift = 0.01
HALO = 4
MOMENTS = 6
NORM_FLOOR = 1e-14

VMEM = pl.BlockSpec(memory_space=pltpu.VMEM)
HBM = pl.BlockSpec(memory_space=pltpu.HBM)
PARAMS = pltpu.CompilerParams(vmem_limit_bytes=8 * 2**20)


def tile_iota(axis):
    return lax.broadcasted_iota(jnp.int32, (8, 128), axis)


def y_next(tile):
    return pltpu.roll(tile, 127, 1)


def y_prev(tile):
    return pltpu.roll(tile, 1, 1)


def z_next(pair):
    last = tile_iota(0) == 7
    first, second = (pltpu.roll(tile, 7, 0) for tile in pair)
    return jnp.where(last, second, first), jnp.where(last, first, second)


def z_prev(pair):
    top = tile_iota(0) == 0
    first, second = (pltpu.roll(tile, 1, 0) for tile in pair)
    return jnp.where(top, second, first), jnp.where(top, first, second)


def parity(axis):
    return lax.rem(lax.axis_index(axis), 2)


def choose(odd, if_even, if_odd):
    return jnp.where(jnp.full((8, 128), odd, jnp.int32) == 0, if_even, if_odd)


def prepare(
    labels_hbm, table_hbm, factor_hbm, chi_hbm, weights_hbm, own, x_a, x_b, z_a, z_b, splat,
    labels, table, factor, weights, sems,
):
    odd_col = parity("col")
    moves = [(chi_hbm.at[j], own.at[j]) for j in range(3)] + [(factor_hbm, factor), (labels_hbm, labels)]
    moves += [(table_hbm, table), (weights_hbm, weights)]
    copies = [pltpu.make_async_copy(source, target, sems.at[n]) for n, (source, target) in enumerate(moves)]
    for copy in copies:
        copy.start()
    odd_slab = parity("slab")
    half = tile_iota(0) < 4

    def fill(f):
        for x in range(HALO):
            low, high = own[f, x], own[f, HALO + x]
            x_a[f, x] = choose(odd_col, high, low)
            x_b[f, x] = choose(odd_col, low, high)
        for i in range(HALO):
            even, odd = own[f, 2 * i], own[f, 2 * i + 1]
            low_rows = jnp.where(half, even, pltpu.roll(odd, 4, 0))
            high_rows = jnp.where(half, pltpu.roll(even, 4, 0), odd)
            z_a[f, i] = choose(odd_slab, high_rows, low_rows)
            z_b[f, i] = choose(odd_slab, low_rows, high_rows)

    for f in range(3):
        copies[f].wait()
        fill(f)
    for copy in copies[3:]:
        copy.wait()
    for x in range(2 * HALO):
        label = labels[x]
        own[3, x] = jnp.where(label == 0, table[0], jnp.where(label == 1, table[1], table[2])) * factor[x]
    fill(3)
    for i in range(3):
        for j in range(3):
            splat[3 * i + j] = jnp.full((8, 128), weights[i, j], jnp.float32)


def fold(z_b, z_a, ring, corner_a, corner_b):
    odd_col, odd_slab = parity("col"), parity("slab")
    half = tile_iota(0) < 4
    outer = (tile_iota(0) < 2) | (tile_iota(0) >= 6)

    def packed(first, second, third):
        return first, jnp.where(outer, second, jnp.where(half, pltpu.roll(third, 2, 0), pltpu.roll(third, 6, 0)))

    for f in range(4):
        tiles = []
        for i in range(HALO):
            up, down = choose(odd_slab, z_a[f, i], z_b[f, i]), choose(odd_slab, z_b[f, i], z_a[f, i])
            tiles.append(jnp.where(half, up, pltpu.roll(down, 4, 0)))
            tiles.append(jnp.where(half, pltpu.roll(up, 4, 0), down))
        for x, tile in enumerate(tiles):
            ring[f, x] = tile
        for n, (low, high) in enumerate(zip(packed(*tiles[:3]), packed(*tiles[:-4:-1]))):
            corner_a[f, n] = choose(odd_col, high, low)
            corner_b[f, n] = choose(odd_col, low, high)


def two_sum(a, b):
    total = a + b
    part = total - a
    return total, (a - (total - part)) + (b - part)


def split(value):
    scaled = 4097.0 * value
    top = scaled - (scaled - value)
    return top, value - top


def exact_product(a, a_parts, b, b_parts):
    product = a * b
    (a_top, a_rest), (b_top, b_rest) = a_parts, b_parts
    return product, ((a_top * b_top - product) + a_top * b_rest + a_rest * b_top) + a_rest * b_rest


def two_product(a, b):
    return exact_product(a, split(a), b, split(b))


def pair_sum(a, b):
    total, error = two_sum(a[0], b[0])
    return total, error + (a[1] + b[1])


def pair_product(a, b):
    product, error = two_product(a[0], b[0])
    return product, error + (a[0] * b[1] + a[1] * b[0])


def total_row(pairs):
    row = tile_iota(0)
    lane = tile_iota(1)
    place = [[n] for n in range(len(pairs))]
    for width in (4, 2, 1):
        lower = (row & width) == 0
        merged, spots = [], []
        for n in range(0, len(pairs), 2):
            first, second = pairs[n], pairs[min(n + 1, len(pairs) - 1)]
            kept = [jnp.where(lower, a, b) for a, b in zip(first, second)]
            moved = [jnp.where(lower, pltpu.roll(a, 8 - width, 0), pltpu.roll(b, width, 0)) for a, b in zip(first, second)]
            merged.append(pair_sum(kept, moved))
            spots.append((place[n], place[n + 1] if n + 1 < len(pairs) else None))
        pairs, place = merged, spots
    result = jnp.zeros((8, 128), jnp.float32)

    def home(spot, at, width):
        if spot is None:
            return
        if len(spot) == 1:
            yield spot[0], at
            return
        yield from home(spot[0], at, 2 * width)
        yield from home(spot[1], at + width, 2 * width)

    for pair, spot in zip(pairs, place):
        for shift in (64, 32, 16, 8, 4, 2, 1):
            pair = pair_sum(pair, [pltpu.roll(a, shift, 1) for a in pair])
        for n, at in home(spot, 0, 1):
            result = jnp.where((row == at) & (lane == 4 * n), pair[0], result)
            result = jnp.where((row == at) & (lane == 4 * n + 1), pair[1], result)
    return jnp.sum(result, axis=0, keepdims=True)


LAYERS = 2 * HALO
TOTAL = 2 * LAYERS


PAIRS = ((0, 0), (0, 1), (1, 1), (1, 2), (2, 2), (2, 3))


def needed(k, t):
    return range(1 + k + t, TOTAL - 1 - k - t)


def inner(k, t):
    return range(HALO + k + t, HALO + LAYERS - k - t)


def harmonic(here, after):
    return 2.0 * here * after / (here + after)


def keep_y(cond, x, t, here):
    value = harmonic(here, y_next(here))
    cond[2, x, t] = value
    cond[4, x, t] = y_prev(value)


def keep_z(cond, x, here):
    values = [harmonic(tile, beside) for tile, beside in zip(here, z_next(here))]
    for t, before in enumerate(z_prev(values)):
        cond[1, x, t] = values[t]
        cond[3, x, t] = before


def out_flow(x, tiles, value, cond, offset, fluxes):
    def x_flux(face, t):
        if (face, t) not in fluxes:
            fluxes[face, t] = cond(0, face, t) * (offset[0] + (value(face + 1, t) - value(face, t)))
        return fluxes[face, t]

    here = [value(x, t) for t in range(2)]
    above, below = z_next(here), z_prev(here)
    added = {}
    for t in tiles:
        z_part = cond(3, x, t) * (offset[1] + (here[t] - below[t])) - cond(1, x, t) * (offset[1] + (above[t] - here[t]))
        y_part = cond(4, x, t) * (offset[2] + (here[t] - y_prev(here[t]))) - cond(2, x, t) * (
            offset[2] + (y_next(here[t]) - here[t])
        )
        added[t] = (x_flux(x - 1, t) - x_flux(x, t)) + z_part + y_part
    return added


def both(read, *index):
    return [read(*index, t) for t in range(2)]


def by_layer(wanted):
    for x in range(TOTAL):
        tiles = [t for t in range(2) if wanted(x, t)]
        if tiles:
            yield x, tiles


def add_source(wanted, grid, cond, splat, field):
    offset = [[1.0 if d == j else 0.0 for d in range(3)] for j in range(3)]
    fluxes = [{} for _ in range(3)]
    for x, tiles in by_layer(wanted):
        drive = [
            out_flow(x, tiles, functools.partial(grid, j), cond, offset[j], fluxes[j]) for j in range(3)
        ]
        for i in range(3):
            for t in tiles:
                field[0, i, x, t] = (
                    splat[3 * i] * drive[0][t] + splat[3 * i + 1] * drive[1][t] + splat[3 * i + 2] * drive[2][t]
                )


def applied(k, i, wanted, v, cond):
    fluxes = {}
    value = functools.partial(v, k, i)
    for x, tiles in by_layer(wanted):
        added = out_flow(x, tiles, value, cond, (0.0, 0.0, 0.0), fluxes)
        yield x, {t: mass_shift * value(x, t) + added[t] for t in tiles}


def add_moments(partial, wanted, v, last):
    for i in range(3):
        for x in range(HALO, HALO + LAYERS):
            pairs = [(m, pair) for m, pair in enumerate(PAIRS) if wanted(pair[1], x)]
            used = sorted({k for m, pair in pairs for k in pair})
            tiles = {k: last[i, x] if k == 3 else v(k, i, x, 0) for k in used}
            parts = {k: split(tiles[k]) for k in used}
            for m, (a, b) in pairs:
                product = exact_product(tiles[a], parts[a], tiles[b], parts[b])
                key = 3 * m + i
                partial[key] = pair_sum(partial[key], product) if key in partial else product


def face_parts(d, here, after, chi_here, chi_after, splat):
    local = [(1.0 if j == d else 0.0) + (chi_after[j] - chi_here[j]) for j in range(3)]
    energy = None
    for i in range(3):
        part = local[i] * (splat[3 * i] * local[0] + splat[3 * i + 1] * local[1] + splat[3 * i + 2] * local[2])
        energy = part if energy is None else energy + part
    inverse = 1.0 / (here + after)
    share = after * inverse
    rest = here * inverse
    now, back = 2.0 * share * share, 2.0 * rest * rest
    return [energy * now] + [value * now for value in local], [energy * back] + [value * back for value in local]


def early(own, ring, x_b, x_a, splat, halo, cond, field, base, slopes, moments):
    odd_col = parity("col")
    for f in range(4):
        for n in range(HALO):
            halo[f, n] = choose(odd_col, x_b[f, n], x_a[f, n])
            halo[f, HALO + n] = choose(odd_col, x_a[f, n], x_b[f, n])

    def grid(f, x, t):
        if t == 1:
            return ring[f, x - HALO]
        if x < HALO:
            return halo[f, x]
        return own[f, x - HALO] if x < HALO + LAYERS else halo[f, x - LAYERS]

    for x in range(TOTAL):
        here = grid(3, x, 0)
        keep_y(cond, x, 0, here)
        if x + 1 < TOTAL:
            cond[0, x, 0] = harmonic(here, grid(3, x + 1, 0))
        if HALO <= x < HALO + LAYERS:
            other = grid(3, x, 1)
            keep_y(cond, x, 1, other)
            if x + 1 < HALO + LAYERS:
                cond[0, x, 1] = harmonic(other, grid(3, x + 1, 1))
            keep_z(cond, x, (here, other))

    def ready(*index):
        return cond[index]

    def v(*index):
        return field[index]

    add_source(lambda x, t: x in inner(0, t), grid, ready, splat, field)
    for k in (1, 2):
        for i in range(3):
            for x, value in applied(k - 1, i, lambda x, t: x in inner(k, t), v, ready):
                for t in value:
                    field[k, i, x, t] = value[t]
    last = {}
    for i in range(3):
        for x, value in applied(2, i, lambda x, t: t == 0 and x in inner(3, 0), v, ready):
            last[i, x] = value[0]
    partial = {}
    add_moments(partial, lambda k, x: x in inner(k, 0), v, last)
    for n, pair in partial.items():
        moments[0, n], moments[1, n] = pair

    carried = None
    for x in range(HALO - 1, HALO + LAYERS):
        here, after = [[grid(f, n, 0) for f in range(4)] for n in (x, x + 1)]
        now, back = face_parts(0, here[3], after[3], here[:3], after[:3], splat)
        if carried is not None:
            beside = [y_next(tile) for tile in here]
            y_now, y_back = face_parts(2, here[3], beside[3], here[:3], beside[:3], splat)
            y_back = [y_prev(tile) for tile in y_back]
            pairs = [(here[f], grid(f, x, 1)) for f in range(4)]
            nexts = [z_next(pair) for pair in pairs]
            z_now, z_back = zip(
                *[
                    face_parts(1, pairs[3][t], nexts[3][t], [p[t] for p in pairs[:3]], [p[t] for p in nexts[:3]], splat)
                    for t in range(2)
                ]
            )
            z_now, z_back = z_now[0], [z_prev(pair)[0] for pair in zip(*z_back)]
            sides = ((now, carried), (z_now, z_back), (y_now, y_back))
            base[x - HALO] = sum(side[0] for pair in sides for side in pair)
            for d in range(3):
                for n in range(2):
                    for j in range(3):
                        slopes[d, n, j, x - HALO] = sides[d][n][1 + j]
        carried = back


def krylov(
    peers, own, z_ring, halo, corner_b, corner_a, splat, early_cond, early_field, moments, field, sums, ring, cond
):
    odd_col = parity("col")
    half = tile_iota(0) < 4
    for f in range(4):
        tiles = [(corner_a[f, n], corner_b[f, n]) for n in range(2)]
        low = [choose(odd_col, b, a) for a, b in tiles]
        high = [choose(odd_col, a, b) for a, b in tiles]
        for (first, shared), spots in ((low, (3, 2, 1, 0)), (high, (4, 5, 6, 7))):
            third = jnp.where(half, pltpu.roll(shared, 6, 0), pltpu.roll(shared, 2, 0))
            for spot, tile in zip(spots, (first, shared, third, third)):
                ring[f, spot] = tile

    def grid(f, x, t):
        if x < HALO:
            return (halo, ring)[t][f, x]
        if x < HALO + LAYERS:
            return (own, z_ring)[t][f, x - HALO]
        return (halo, ring)[t][f, x - LAYERS]

    def is_early(d, x, t):
        return HALO <= x < HALO + LAYERS - (1 if d == 0 and t == 1 else 0) or (t == 0 and d in (0, 2, 4))

    def ready(d, x, t):
        return (early_cond if is_early(d, x, t) else cond)[d, x, t]

    def v(k, i, x, t):
        return (early_field if x in inner(k, t) else field)[k, i, x, t]

    for x in range(1, TOTAL - 1):
        if x < TOTAL - 2 and not is_early(0, x, 1):
            cond[0, x, 1] = harmonic(grid(3, x, 1), grid(3, x + 1, 1))
        if x in needed(0, 1) and not is_early(2, x, 1):
            keep_y(cond, x, 1, grid(3, x, 1))
        if not is_early(1, x, 1):
            keep_z(cond, x, both(grid, 3, x))

    add_source(lambda x, t: x in needed(0, t) and x not in inner(0, t), grid, ready, splat, field)
    for k in (1, 2):
        for i in range(3):
            for x, value in applied(k - 1, i, lambda x, t: x in needed(k, t) and x not in inner(k, t), v, ready):
                for t in value:
                    field[k, i, x, t] = value[t]
    last = {}
    for i in range(3):
        for x, value in applied(2, i, lambda x, t: t == 0 and x in needed(3, 0) and x not in inner(3, 0), v, ready):
            last[i, x] = value[0]
    partial = {n: (moments[0, n], moments[1, n]) for n in range(3 * MOMENTS)}
    add_moments(partial, lambda k, x: x not in inner(k, 0), v, last)
    sums[...] = jnp.broadcast_to(total_row([partial[n] for n in range(3 * MOMENTS)]), (peers, 128))


def quadratic(terms):
    products = [pair_product(a, b) for a, b in terms]
    total = products[0]
    for product in products[1:]:
        total = pair_sum(total, product)
    return total[0] + total[1]


def coefficients(sums):
    count = sums.shape[0] // 8
    pairs = [(sums[8 * n : 8 * n + 8], jnp.zeros((8, 128), jnp.float32)) for n in range(count)]
    while len(pairs) > 1:
        tail = pairs[len(pairs) // 2 * 2 :]
        pairs = [pair_sum(pairs[n], pairs[n + 1]) for n in range(0, len(pairs) - 1, 2)] + tail
    pair = pairs[0]
    for shift in (4, 2, 1):
        pair = pair_sum(pair, [pltpu.roll(a, shift, 0) for a in pair])
    value, error = pair[0], pair[1] + pltpu.roll(pair[0], 127, 1)

    def moment(m):
        if m == 0:
            return value, error
        return pltpu.roll(value, 128 - 12 * m, 1), pltpu.roll(error, 128 - 12 * m, 1)

    m0, m1, m2, m3, m4, m5 = [moment(m) for m in range(MOMENTS)]
    none = jnp.zeros((8, 128), jnp.float32)
    one = (jnp.ones((8, 128), jnp.float32), none)
    alpha0 = m0[0] / m1[0]
    inverse0 = 1.0 / m0[0]
    alpha0_squared = two_product(alpha0, alpha0)
    norm1 = quadratic(((one, m0), ((-2.0 * alpha0, none), m1), (alpha0_squared, m2)))
    norm1 = jnp.maximum(norm1, NORM_FLOOR * m0[0])
    inverse1 = 1.0 / norm1
    grow = 1.0 + norm1 * inverse0
    curve1 = quadratic(
        ((two_product(grow, grow), m1), (two_product(-2.0 * grow, alpha0), m2), (alpha0_squared, m3))
    )
    alpha1 = norm1 / jnp.maximum(curve1, mass_shift * norm1)
    r1 = -(alpha0 + alpha1 * grow)
    r2 = alpha1 * alpha0
    norm2 = quadratic(
        (
            (one, m0),
            ((2.0 * r1, none), m1),
            (pair_sum(two_product(r1, r1), (2.0 * r2, none)), m2),
            (two_product(2.0 * r1, r2), m3),
            (two_product(r2, r2), m4),
        )
    )
    norm2 = jnp.maximum(norm2, NORM_FLOOR * norm1)
    beta1 = norm2 * inverse1
    p0, p1, p2 = 1.0 + beta1 * grow, r1 - beta1 * alpha0, r2
    curve2 = quadratic(
        (
            (two_product(p0, p0), m1),
            (two_product(2.0 * p0, p1), m2),
            (pair_sum(two_product(p1, p1), two_product(2.0 * p0, p2)), m3),
            (two_product(2.0 * p1, p2), m4),
            (two_product(p2, p2), m5),
        )
    )
    alpha2 = norm2 / jnp.maximum(curve2, mass_shift * norm2)
    return alpha0 + alpha1 * grow + alpha2 * p0, alpha2 * p1 - alpha1 * alpha0, alpha2 * p2


def finish(sums, early_field, field, base, slopes, adjoint_hbm, gradient_hbm, adjoint, gradient, lam, sems):
    lane = tile_iota(1)
    copies = []
    scale = []
    for c in coefficients(sums):
        scale.append([jnp.sum(jnp.where(lane == 4 * i, c, 0.0), axis=1, keepdims=True) for i in range(3)])
    for i in range(3):
        for x in range(LAYERS + 2):
            for t in range(2):
                if t == 1 and x in (0, LAYERS + 1):
                    continue
                at = x + HALO - 1
                v = [(early_field if at in inner(k, t) else field)[k, i, at, t] for k in range(3)]
                value = scale[0][i] * v[0] + scale[1][i] * v[1] + scale[2][i] * v[2]
                lam[i, x, t] = value
                if t == 0 and 0 < x <= LAYERS:
                    adjoint[i, x - 1] = value
        copies.append(pltpu.make_async_copy(adjoint.at[i], adjoint_hbm.at[i], sems.at[i]))
        copies[-1].start()

    for x in range(1, LAYERS + 1):
        total = base[x - 1]
        for j in range(3):
            pair = (lam[j, x, 0], lam[j, x, 1])
            here = pair[0]
            around = (
                (lam[j, x + 1, 0], lam[j, x - 1, 0]),
                (z_next(pair)[0], z_prev(pair)[0]),
                (y_next(here), y_prev(here)),
            )
            for d, (after, before) in enumerate(around):
                total = total - (after - here) * slopes[d, 0, j, x - 1] - (here - before) * slopes[d, 1, j, x - 1]
        gradient[x - 1] = total
        if x % HALO == 0:
            part = pl.ds(x - HALO, HALO)
            copies.append(pltpu.make_async_copy(gradient.at[part], gradient_hbm.at[part], sems.at[2 + x // HALO]))
            copies[-1].start()
    for copy in copies:
        copy.wait()


def swap_a(axis):
    return [(i, i ^ 1) for i in range(lax.axis_size(axis))]


def swap_b(axis):
    count = lax.axis_size(axis)
    return [(i, (i + 1 if i % 2 else i - 1) % count) for i in range(count)]


def in_hbm(*arrays):
    return [pltpu.with_memory_space_constraint(a, pltpu.HBM) for a in arrays]


def shards(labels, table, factor, chi, weights):
    assert factor.shape == (LAYERS, 8, 128)
    assert lax.axis_size("col") % 2 == 0 and lax.axis_size("slab") % 2 == 0
    peers = lax.axis_size("col") * lax.axis_size("slab")
    f32 = functools.partial(jax.ShapeDtypeStruct, dtype=jnp.float32)
    scratch = functools.partial(pltpu.VMEM, dtype=jnp.float32)
    block = (4, LAYERS, 8, 128)
    half_block = f32((4, HALO, 8, 128))
    corner = f32((4, 2, 8, 128))
    fields = f32((3, 3, TOTAL, 2, 8, 128))

    own, x_a, x_b, z_a, z_b, splat = pl.pallas_call(
        prepare,
        out_shape=(f32(block),) + (half_block,) * 4 + (f32((9, 8, 128)),),
        in_specs=[HBM] * 5,
        out_specs=(VMEM,) * 6,
        scratch_shapes=[
            pltpu.VMEM((LAYERS, 8, 128), jnp.int32),
            pltpu.SMEM((3,), jnp.float32),
            scratch((LAYERS, 8, 128)),
            pltpu.SMEM((3, 3), jnp.float32),
            pltpu.SemaphoreType.DMA((12,)),
        ],
        compiler_params=PARAMS,
        name="prepare",
    )(*in_hbm(labels, table, factor, chi, weights))

    z_b = lax.ppermute(z_b, "slab", swap_b("slab"))
    z_a = lax.ppermute(z_a, "slab", swap_a("slab"))
    x_b = lax.ppermute(x_b, "col", swap_b("col"))
    x_a = lax.ppermute(x_a, "col", swap_a("col"))

    ring, corner_a, corner_b = pl.pallas_call(
        fold,
        out_shape=(f32(block), corner, corner),
        in_specs=[VMEM] * 2,
        out_specs=(VMEM,) * 3,
        compiler_params=PARAMS,
        name="fold",
    )(z_b, z_a)
    corner_b = lax.ppermute(corner_b, "col", swap_b("col"))
    corner_a = lax.ppermute(corner_a, "col", swap_a("col"))

    halo, cond, early_field, base, slopes, moments = pl.pallas_call(
        early,
        out_shape=(
            f32(block),
            f32((5, TOTAL, 2, 8, 128)),
            fields,
            f32((LAYERS, 8, 128)),
            f32((3, 2, 3, LAYERS, 8, 128)),
            f32((2, 3 * MOMENTS, 8, 128)),
        ),
        in_specs=[VMEM] * 5,
        out_specs=(VMEM,) * 6,
        compiler_params=PARAMS,
        name="early",
    )(own, ring, x_b, x_a, splat)

    field, sums = pl.pallas_call(
        functools.partial(krylov, peers),
        out_shape=(fields, f32((peers, 128))),
        in_specs=[VMEM] * 9,
        out_specs=(VMEM,) * 2,
        scratch_shapes=[scratch(block), scratch((5, TOTAL, 2, 8, 128))],
        compiler_params=PARAMS,
        name="krylov",
    )(own, ring, halo, corner_b, corner_a, splat, cond, early_field, moments)

    gathered = lax.all_to_all(sums, ("col", "slab"), 0, 0, tiled=True)

    return pl.pallas_call(
        finish,
        out_shape=(f32((3, LAYERS, 8, 128)), f32((LAYERS, 8, 128))),
        in_specs=[VMEM] * 5,
        out_specs=(HBM,) * 2,
        scratch_shapes=[
            scratch((3, LAYERS, 8, 128)),
            scratch((LAYERS, 8, 128)),
            scratch((3, LAYERS + 2, 2, 8, 128)),
            pltpu.SemaphoreType.DMA((5,)),
        ],
        compiler_params=PARAMS,
        name="finish",
    )(gathered, early_field, field, base, slopes)


def solution(mesh):
    in_specs = (
        P("col", "slab", None),
        P(),
        P("col", "slab", None),
        P(None, "col", "slab", None),
        P(),
    )
    out_specs = (P(None, "col", "slab", None), P("col", "slab", None))
    return jax.shard_map(shards, mesh=mesh, in_specs=in_specs, out_specs=out_specs, check_vma=False)
```

```python
import functools

import jax
import jax.numpy as jnp
from jax import lax
from jax.experimental import pallas as pl
from jax.experimental.pallas import tpu as pltpu
from jax.sharding import PartitionSpec as P


mass_shift = 0.01
HALO = 4
MOMENTS = 6
NORM_FLOOR = 1e-14

VMEM = pl.BlockSpec(memory_space=pltpu.VMEM)
HBM = pl.BlockSpec(memory_space=pltpu.HBM)
PARAMS = pltpu.CompilerParams(vmem_limit_bytes=8 * 2**20)


def tile_iota(axis):
    return lax.broadcasted_iota(jnp.int32, (8, 128), axis)


def y_next(tile):
    return pltpu.roll(tile, 127, 1)


def y_prev(tile):
    return pltpu.roll(tile, 1, 1)


def z_next(pair):
    last = tile_iota(0) == 7
    first, second = (pltpu.roll(tile, 7, 0) for tile in pair)
    return jnp.where(last, second, first), jnp.where(last, first, second)


def z_prev(pair):
    top = tile_iota(0) == 0
    first, second = (pltpu.roll(tile, 1, 0) for tile in pair)
    return jnp.where(top, second, first), jnp.where(top, first, second)


def parity(axis):
    return lax.rem(lax.axis_index(axis), 2)


def choose(odd, if_even, if_odd):
    return jnp.where(jnp.full((8, 128), odd, jnp.int32) == 0, if_even, if_odd)


def prepare(
    labels_hbm, table_hbm, factor_hbm, chi_hbm, weights_hbm, own, x_a, x_b, z_a, z_b, splat,
    labels, table, factor, weights, sems,
):
    odd_col = parity("col")
    moves = [(chi_hbm.at[j], own.at[j]) for j in range(3)] + [(factor_hbm, factor), (labels_hbm, labels)]
    moves += [(table_hbm, table), (weights_hbm, weights)]
    copies = [pltpu.make_async_copy(source, target, sems.at[n]) for n, (source, target) in enumerate(moves)]
    for copy in copies:
        copy.start()
    odd_slab = parity("slab")
    half = tile_iota(0) < 4

    def fill(f):
        for x in range(HALO):
            low, high = own[f, x], own[f, HALO + x]
            x_a[f, x] = choose(odd_col, high, low)
            x_b[f, x] = choose(odd_col, low, high)
        for i in range(HALO):
            even, odd = own[f, 2 * i], own[f, 2 * i + 1]
            low_rows = jnp.where(half, even, pltpu.roll(odd, 4, 0))
            high_rows = jnp.where(half, pltpu.roll(even, 4, 0), odd)
            z_a[f, i] = choose(odd_slab, high_rows, low_rows)
            z_b[f, i] = choose(odd_slab, low_rows, high_rows)

    for f in range(3):
        copies[f].wait()
        fill(f)
    for copy in copies[3:]:
        copy.wait()
    for x in range(2 * HALO):
        label = labels[x]
        own[3, x] = jnp.where(label == 0, table[0], jnp.where(label == 1, table[1], table[2])) * factor[x]
    fill(3)
    for i in range(3):
        for j in range(3):
            splat[3 * i + j] = jnp.full((8, 128), weights[i, j], jnp.float32)


def fold(z_b, z_a, ring, corner_a, corner_b):
    odd_col, odd_slab = parity("col"), parity("slab")
    half = tile_iota(0) < 4
    outer = (tile_iota(0) < 2) | (tile_iota(0) >= 6)

    def packed(first, second, third):
        return first, jnp.where(outer, second, jnp.where(half, pltpu.roll(third, 2, 0), pltpu.roll(third, 6, 0)))

    for f in range(4):
        tiles = []
        for i in range(HALO):
            up, down = choose(odd_slab, z_a[f, i], z_b[f, i]), choose(odd_slab, z_b[f, i], z_a[f, i])
            tiles.append(jnp.where(half, up, pltpu.roll(down, 4, 0)))
            tiles.append(jnp.where(half, pltpu.roll(up, 4, 0), down))
        for x, tile in enumerate(tiles):
            ring[f, x] = tile
        for n, (low, high) in enumerate(zip(packed(*tiles[:3]), packed(*tiles[:-4:-1]))):
            corner_a[f, n] = choose(odd_col, high, low)
            corner_b[f, n] = choose(odd_col, low, high)


def two_sum(a, b):
    total = a + b
    part = total - a
    return total, (a - (total - part)) + (b - part)


def split(value):
    scaled = 4097.0 * value
    top = scaled - (scaled - value)
    return top, value - top


def exact_product(a, a_parts, b, b_parts):
    product = a * b
    (a_top, a_rest), (b_top, b_rest) = a_parts, b_parts
    return product, ((a_top * b_top - product) + a_top * b_rest + a_rest * b_top) + a_rest * b_rest


def two_product(a, b):
    return exact_product(a, split(a), b, split(b))


def pair_sum(a, b):
    total, error = two_sum(a[0], b[0])
    return total, error + (a[1] + b[1])


def pair_product(a, b):
    product, error = two_product(a[0], b[0])
    return product, error + (a[0] * b[1] + a[1] * b[0])


def total_row(pairs, start):
    row = tile_iota(0)
    lane = tile_iota(1)
    place = [[n] for n in range(len(pairs))]
    for width in (4, 2, 1):
        lower = (row & width) == 0
        merged, spots = [], []
        for n in range(0, len(pairs), 2):
            first, second = pairs[n], pairs[min(n + 1, len(pairs) - 1)]
            kept = [jnp.where(lower, a, b) for a, b in zip(first, second)]
            moved = [jnp.where(lower, pltpu.roll(a, 8 - width, 0), pltpu.roll(b, width, 0)) for a, b in zip(first, second)]
            merged.append(pair_sum(kept, moved))
            spots.append((place[n], place[n + 1] if n + 1 < len(pairs) else None))
        pairs, place = merged, spots
    result = jnp.zeros((8, 128), jnp.float32)

    def home(spot, at, width):
        if spot is None:
            return
        if len(spot) == 1:
            yield spot[0], at
            return
        yield from home(spot[0], at, 2 * width)
        yield from home(spot[1], at + width, 2 * width)

    for pair, spot in zip(pairs, place):
        for shift in (64, 32, 16, 8, 4, 2, 1):
            pair = pair_sum(pair, [pltpu.roll(a, shift, 1) for a in pair])
        for n, at in home(spot, 0, 1):
            result = jnp.where((row == at) & (lane == 4 * (start + n)), pair[0], result)
            result = jnp.where((row == at) & (lane == 4 * (start + n) + 1), pair[1], result)
    return jnp.sum(result, axis=0, keepdims=True)


LAYERS = 2 * HALO
TOTAL = 2 * LAYERS


PAIRS = ((0, 0), (0, 1), (1, 1), (1, 2), (2, 2), (2, 3))


def needed(k, t):
    return range(1 + k + t, TOTAL - 1 - k - t)


def inner(k, t):
    return range(HALO + k + t, HALO + LAYERS - k - t)


def harmonic(here, after):
    return 2.0 * here * after / (here + after)


def keep_y(cond, x, t, here):
    value = harmonic(here, y_next(here))
    cond[2, x, t] = value
    cond[4, x, t] = y_prev(value)


def keep_z(cond, x, here):
    values = [harmonic(tile, beside) for tile, beside in zip(here, z_next(here))]
    for t, before in enumerate(z_prev(values)):
        cond[1, x, t] = values[t]
        cond[3, x, t] = before


def out_flow(x, tiles, value, cond, offset, fluxes):
    def x_flux(face, t):
        if (face, t) not in fluxes:
            fluxes[face, t] = cond(0, face, t) * (offset[0] + (value(face + 1, t) - value(face, t)))
        return fluxes[face, t]

    here = [value(x, t) for t in range(2)]
    above, below = z_next(here), z_prev(here)
    added = {}
    for t in tiles:
        z_part = cond(3, x, t) * (offset[1] + (here[t] - below[t])) - cond(1, x, t) * (offset[1] + (above[t] - here[t]))
        y_part = cond(4, x, t) * (offset[2] + (here[t] - y_prev(here[t]))) - cond(2, x, t) * (
            offset[2] + (y_next(here[t]) - here[t])
        )
        added[t] = (x_flux(x - 1, t) - x_flux(x, t)) + z_part + y_part
    return added


def both(read, *index):
    return [read(*index, t) for t in range(2)]


def by_layer(wanted):
    for x in range(TOTAL):
        tiles = [t for t in range(2) if wanted(x, t)]
        if tiles:
            yield x, tiles


def add_source(wanted, grid, cond, splat, field):
    offset = [[1.0 if d == j else 0.0 for d in range(3)] for j in range(3)]
    fluxes = [{} for _ in range(3)]
    for x, tiles in by_layer(wanted):
        drive = [
            out_flow(x, tiles, functools.partial(grid, j), cond, offset[j], fluxes[j]) for j in range(3)
        ]
        for i in range(3):
            for t in tiles:
                field[0, i, x, t] = (
                    splat[3 * i] * drive[0][t] + splat[3 * i + 1] * drive[1][t] + splat[3 * i + 2] * drive[2][t]
                )


def applied(k, i, wanted, v, cond):
    fluxes = {}
    value = functools.partial(v, k, i)
    for x, tiles in by_layer(wanted):
        added = out_flow(x, tiles, value, cond, (0.0, 0.0, 0.0), fluxes)
        yield x, {t: mass_shift * value(x, t) + added[t] for t in tiles}


def add_moments(partial, wanted, v, last):
    for i in range(3):
        for x in range(HALO, HALO + LAYERS):
            pairs = [(m, pair) for m, pair in enumerate(PAIRS) if wanted(pair[1], x)]
            used = sorted({k for m, pair in pairs for k in pair})
            tiles = {k: last[i, x] if k == 3 else v(k, i, x, 0) for k in used}
            parts = {k: split(tiles[k]) for k in used}
            for m, (a, b) in pairs:
                product = exact_product(tiles[a], parts[a], tiles[b], parts[b])
                key = 3 * m + i
                partial[key] = pair_sum(partial[key], product) if key in partial else product


def face_parts(d, here, after, chi_here, chi_after, splat):
    local = [(1.0 if j == d else 0.0) + (chi_after[j] - chi_here[j]) for j in range(3)]
    energy = None
    for i in range(3):
        part = local[i] * (splat[3 * i] * local[0] + splat[3 * i + 1] * local[1] + splat[3 * i + 2] * local[2])
        energy = part if energy is None else energy + part
    inverse = 1.0 / (here + after)
    share = after * inverse
    rest = here * inverse
    now, back = 2.0 * share * share, 2.0 * rest * rest
    return [energy * now] + [value * now for value in local], [energy * back] + [value * back for value in local]


def early(own, ring, x_b, x_a, splat, halo, cond, field, base, slopes, moments):
    odd_col = parity("col")
    for f in range(4):
        for n in range(HALO):
            halo[f, n] = choose(odd_col, x_b[f, n], x_a[f, n])
            halo[f, HALO + n] = choose(odd_col, x_a[f, n], x_b[f, n])

    def grid(f, x, t):
        if t == 1:
            return ring[f, x - HALO]
        if x < HALO:
            return halo[f, x]
        return own[f, x - HALO] if x < HALO + LAYERS else halo[f, x - LAYERS]

    for x in range(TOTAL):
        here = grid(3, x, 0)
        keep_y(cond, x, 0, here)
        if x + 1 < TOTAL:
            cond[0, x, 0] = harmonic(here, grid(3, x + 1, 0))
        if HALO <= x < HALO + LAYERS:
            other = grid(3, x, 1)
            keep_y(cond, x, 1, other)
            if x + 1 < HALO + LAYERS:
                cond[0, x, 1] = harmonic(other, grid(3, x + 1, 1))
            keep_z(cond, x, (here, other))

    def ready(*index):
        return cond[index]

    def v(*index):
        return field[index]

    add_source(lambda x, t: x in inner(0, t), grid, ready, splat, field)
    for k in (1, 2):
        for i in range(3):
            for x, value in applied(k - 1, i, lambda x, t: x in inner(k, t), v, ready):
                for t in value:
                    field[k, i, x, t] = value[t]
    last = {}
    for i in range(3):
        for x, value in applied(2, i, lambda x, t: t == 0 and x in inner(3, 0), v, ready):
            last[i, x] = value[0]
    partial = {}
    add_moments(partial, lambda k, x: x in inner(k, 0), v, last)
    for n, pair in partial.items():
        moments[0, n], moments[1, n] = pair

    carried = None
    for x in range(HALO - 1, HALO + LAYERS):
        here, after = [[grid(f, n, 0) for f in range(4)] for n in (x, x + 1)]
        now, back = face_parts(0, here[3], after[3], here[:3], after[:3], splat)
        if carried is not None:
            beside = [y_next(tile) for tile in here]
            y_now, y_back = face_parts(2, here[3], beside[3], here[:3], beside[:3], splat)
            y_back = [y_prev(tile) for tile in y_back]
            pairs = [(here[f], grid(f, x, 1)) for f in range(4)]
            nexts = [z_next(pair) for pair in pairs]
            z_now, z_back = zip(
                *[
                    face_parts(1, pairs[3][t], nexts[3][t], [p[t] for p in pairs[:3]], [p[t] for p in nexts[:3]], splat)
                    for t in range(2)
                ]
            )
            z_now, z_back = z_now[0], [z_prev(pair)[0] for pair in zip(*z_back)]
            sides = ((now, carried), (z_now, z_back), (y_now, y_back))
            base[x - HALO] = sum(side[0] for pair in sides for side in pair)
            for d in range(3):
                for n in range(2):
                    for j in range(3):
                        slopes[d, n, j, x - HALO] = sides[d][n][1 + j]
        carried = back


def krylov(
    peers, own, z_ring, halo, corner_b, corner_a, splat, early_cond, early_field, moments, field, sums, ring, cond
):
    odd_col = parity("col")
    half = tile_iota(0) < 4
    for f in range(4):
        tiles = [(corner_a[f, n], corner_b[f, n]) for n in range(2)]
        low = [choose(odd_col, b, a) for a, b in tiles]
        high = [choose(odd_col, a, b) for a, b in tiles]
        for (first, shared), spots in ((low, (3, 2, 1, 0)), (high, (4, 5, 6, 7))):
            third = jnp.where(half, pltpu.roll(shared, 6, 0), pltpu.roll(shared, 2, 0))
            for spot, tile in zip(spots, (first, shared, third, third)):
                ring[f, spot] = tile

    def grid(f, x, t):
        if x < HALO:
            return (halo, ring)[t][f, x]
        if x < HALO + LAYERS:
            return (own, z_ring)[t][f, x - HALO]
        return (halo, ring)[t][f, x - LAYERS]

    def is_early(d, x, t):
        return HALO <= x < HALO + LAYERS - (1 if d == 0 and t == 1 else 0) or (t == 0 and d in (0, 2, 4))

    def ready(d, x, t):
        return (early_cond if is_early(d, x, t) else cond)[d, x, t]

    def v(k, i, x, t):
        return (early_field if x in inner(k, t) else field)[k, i, x, t]

    for x in range(1, TOTAL - 1):
        if x < TOTAL - 2 and not is_early(0, x, 1):
            cond[0, x, 1] = harmonic(grid(3, x, 1), grid(3, x + 1, 1))
        if x in needed(0, 1) and not is_early(2, x, 1):
            keep_y(cond, x, 1, grid(3, x, 1))
        if not is_early(1, x, 1):
            keep_z(cond, x, both(grid, 3, x))

    add_source(lambda x, t: x in needed(0, t) and x not in inner(0, t), grid, ready, splat, field)
    for k in (1, 2):
        for i in range(3):
            for x, value in applied(k - 1, i, lambda x, t: x in needed(k, t) and x not in inner(k, t), v, ready):
                for t in value:
                    field[k, i, x, t] = value[t]
    partial = {n: (moments[0, n], moments[1, n]) for n in range(3 * MOMENTS)}
    add_moments(partial, lambda k, x: k < 3 and x not in inner(k, 0), v, None)
    others = 3 * (MOMENTS - 1)
    row = total_row([partial[n] for n in range(others)], 0)
    last = {}
    for i in range(3):
        for x, value in applied(2, i, lambda x, t: t == 0 and x in needed(3, 0) and x not in inner(3, 0), v, ready):
            last[i, x] = value[0]
    add_moments(partial, lambda k, x: k == 3 and x not in inner(k, 0), v, last)
    row = row + total_row([partial[n] for n in range(others, 3 * MOMENTS)], others)
    sums[...] = jnp.broadcast_to(row, (peers, 128))


def quadratic(terms):
    products = [pair_product(a, b) for a, b in terms]
    total = products[0]
    for product in products[1:]:
        total = pair_sum(total, product)
    return total[0] + total[1]


def coefficients(sums):
    count = sums.shape[0] // 8
    pairs = [(sums[8 * n : 8 * n + 8], jnp.zeros((8, 128), jnp.float32)) for n in range(count)]
    while len(pairs) > 1:
        tail = pairs[len(pairs) // 2 * 2 :]
        pairs = [pair_sum(pairs[n], pairs[n + 1]) for n in range(0, len(pairs) - 1, 2)] + tail
    pair = pairs[0]
    for shift in (4, 2, 1):
        pair = pair_sum(pair, [pltpu.roll(a, shift, 0) for a in pair])
    value, error = pair[0], pair[1] + pltpu.roll(pair[0], 127, 1)

    def moment(m):
        if m == 0:
            return value, error
        return pltpu.roll(value, 128 - 12 * m, 1), pltpu.roll(error, 128 - 12 * m, 1)

    m0, m1, m2, m3, m4, m5 = [moment(m) for m in range(MOMENTS)]
    none = jnp.zeros((8, 128), jnp.float32)
    one = (jnp.ones((8, 128), jnp.float32), none)
    alpha0 = m0[0] / m1[0]
    inverse0 = 1.0 / m0[0]
    alpha0_squared = two_product(alpha0, alpha0)
    norm1 = quadratic(((one, m0), ((-2.0 * alpha0, none), m1), (alpha0_squared, m2)))
    norm1 = jnp.maximum(norm1, NORM_FLOOR * m0[0])
    inverse1 = 1.0 / norm1
    grow = 1.0 + norm1 * inverse0
    curve1 = quadratic(
        ((two_product(grow, grow), m1), (two_product(-2.0 * grow, alpha0), m2), (alpha0_squared, m3))
    )
    alpha1 = norm1 / jnp.maximum(curve1, mass_shift * norm1)
    r1 = -(alpha0 + alpha1 * grow)
    r2 = alpha1 * alpha0
    norm2 = quadratic(
        (
            (one, m0),
            ((2.0 * r1, none), m1),
            (pair_sum(two_product(r1, r1), (2.0 * r2, none)), m2),
            (two_product(2.0 * r1, r2), m3),
            (two_product(r2, r2), m4),
        )
    )
    norm2 = jnp.maximum(norm2, NORM_FLOOR * norm1)
    beta1 = norm2 * inverse1
    p0, p1, p2 = 1.0 + beta1 * grow, r1 - beta1 * alpha0, r2
    curve2 = quadratic(
        (
            (two_product(p0, p0), m1),
            (two_product(2.0 * p0, p1), m2),
            (pair_sum(two_product(p1, p1), two_product(2.0 * p0, p2)), m3),
            (two_product(2.0 * p1, p2), m4),
            (two_product(p2, p2), m5),
        )
    )
    alpha2 = norm2 / jnp.maximum(curve2, mass_shift * norm2)
    return alpha0 + alpha1 * grow + alpha2 * p0, alpha2 * p1 - alpha1 * alpha0, alpha2 * p2


def finish(sums, early_field, field, base, slopes, adjoint_hbm, gradient_hbm, adjoint, gradient, lam, sems):
    lane = tile_iota(1)
    copies = []
    scale = []
    for c in coefficients(sums):
        scale.append([jnp.sum(jnp.where(lane == 4 * i, c, 0.0), axis=1, keepdims=True) for i in range(3)])
    for i in range(3):
        for x in range(LAYERS + 2):
            for t in range(2):
                if t == 1 and x in (0, LAYERS + 1):
                    continue
                at = x + HALO - 1
                v = [(early_field if at in inner(k, t) else field)[k, i, at, t] for k in range(3)]
                value = scale[0][i] * v[0] + scale[1][i] * v[1] + scale[2][i] * v[2]
                lam[i, x, t] = value
                if t == 0 and 0 < x <= LAYERS:
                    adjoint[i, x - 1] = value
        copies.append(pltpu.make_async_copy(adjoint.at[i], adjoint_hbm.at[i], sems.at[i]))
        copies[-1].start()

    for x in range(1, LAYERS + 1):
        total = base[x - 1]
        for j in range(3):
            pair = (lam[j, x, 0], lam[j, x, 1])
            here = pair[0]
            around = (
                (lam[j, x + 1, 0], lam[j, x - 1, 0]),
                (z_next(pair)[0], z_prev(pair)[0]),
                (y_next(here), y_prev(here)),
            )
            for d, (after, before) in enumerate(around):
                total = total - (after - here) * slopes[d, 0, j, x - 1] - (here - before) * slopes[d, 1, j, x - 1]
        gradient[x - 1] = total
        if x % HALO == 0:
            part = pl.ds(x - HALO, HALO)
            copies.append(pltpu.make_async_copy(gradient.at[part], gradient_hbm.at[part], sems.at[2 + x // HALO]))
            copies[-1].start()
    for copy in copies:
        copy.wait()


def swap_a(axis):
    return [(i, i ^ 1) for i in range(lax.axis_size(axis))]


def swap_b(axis):
    count = lax.axis_size(axis)
    return [(i, (i + 1 if i % 2 else i - 1) % count) for i in range(count)]


def in_hbm(*arrays):
    return [pltpu.with_memory_space_constraint(a, pltpu.HBM) for a in arrays]


def shards(labels, table, factor, chi, weights):
    assert factor.shape == (LAYERS, 8, 128)
    assert lax.axis_size("col") % 2 == 0 and lax.axis_size("slab") % 2 == 0
    peers = lax.axis_size("col") * lax.axis_size("slab")
    f32 = functools.partial(jax.ShapeDtypeStruct, dtype=jnp.float32)
    scratch = functools.partial(pltpu.VMEM, dtype=jnp.float32)
    block = (4, LAYERS, 8, 128)
    half_block = f32((4, HALO, 8, 128))
    corner = f32((4, 2, 8, 128))
    fields = f32((3, 3, TOTAL, 2, 8, 128))

    own, x_a, x_b, z_a, z_b, splat = pl.pallas_call(
        prepare,
        out_shape=(f32(block),) + (half_block,) * 4 + (f32((9, 8, 128)),),
        in_specs=[HBM] * 5,
        out_specs=(VMEM,) * 6,
        scratch_shapes=[
            pltpu.VMEM((LAYERS, 8, 128), jnp.int32),
            pltpu.SMEM((3,), jnp.float32),
            scratch((LAYERS, 8, 128)),
            pltpu.SMEM((3, 3), jnp.float32),
            pltpu.SemaphoreType.DMA((12,)),
        ],
        compiler_params=PARAMS,
        name="prepare",
    )(*in_hbm(labels, table, factor, chi, weights))

    z_b = lax.ppermute(z_b, "slab", swap_b("slab"))
    z_a = lax.ppermute(z_a, "slab", swap_a("slab"))
    x_b = lax.ppermute(x_b, "col", swap_b("col"))
    x_a = lax.ppermute(x_a, "col", swap_a("col"))

    ring, corner_a, corner_b = pl.pallas_call(
        fold,
        out_shape=(f32(block), corner, corner),
        in_specs=[VMEM] * 2,
        out_specs=(VMEM,) * 3,
        compiler_params=PARAMS,
        name="fold",
    )(z_b, z_a)
    corner_b = lax.ppermute(corner_b, "col", swap_b("col"))
    corner_a = lax.ppermute(corner_a, "col", swap_a("col"))

    halo, cond, early_field, base, slopes, moments = pl.pallas_call(
        early,
        out_shape=(
            f32(block),
            f32((5, TOTAL, 2, 8, 128)),
            fields,
            f32((LAYERS, 8, 128)),
            f32((3, 2, 3, LAYERS, 8, 128)),
            f32((2, 3 * MOMENTS, 8, 128)),
        ),
        in_specs=[VMEM] * 5,
        out_specs=(VMEM,) * 6,
        compiler_params=PARAMS,
        name="early",
    )(own, ring, x_b, x_a, splat)

    field, sums = pl.pallas_call(
        functools.partial(krylov, peers),
        out_shape=(fields, f32((peers, 128))),
        in_specs=[VMEM] * 9,
        out_specs=(VMEM,) * 2,
        scratch_shapes=[scratch(block), scratch((5, TOTAL, 2, 8, 128))],
        compiler_params=PARAMS,
        name="krylov",
    )(own, ring, halo, corner_b, corner_a, splat, cond, early_field, moments)

    gathered = lax.all_to_all(sums, ("col", "slab"), 0, 0, tiled=True)

    return pl.pallas_call(
        finish,
        out_shape=(f32((3, LAYERS, 8, 128)), f32((LAYERS, 8, 128))),
        in_specs=[VMEM] * 5,
        out_specs=(HBM,) * 2,
        scratch_shapes=[
            scratch((3, LAYERS, 8, 128)),
            scratch((LAYERS, 8, 128)),
            scratch((3, LAYERS + 2, 2, 8, 128)),
            pltpu.SemaphoreType.DMA((5,)),
        ],
        compiler_params=PARAMS,
        name="finish",
    )(gathered, early_field, field, base, slopes)


def solution(mesh):
    in_specs = (
        P("col", "slab", None),
        P(),
        P("col", "slab", None),
        P(None, "col", "slab", None),
        P(),
    )
    out_specs = (P(None, "col", "slab", None), P("col", "slab", None))
    return jax.shard_map(shards, mesh=mesh, in_specs=in_specs, out_specs=out_specs, check_vma=False)
```
